32 devices in a mesh: row: 8 (over z, x), col: 4 (over y, core).
Axes of the slice: x: 2, y: 2, z: 4, core: 2. Of those that a mesh axis runs over, the one named last changes fastest.
Arguments:
- suffix_x: bfloat16 [4, 8, 512, 1024], P('col', 'row'), may hold values from -40 to 40
- segment_ids: int32 [4, 8, 512], P('col', 'row'), may hold values from 0 to 3, never falling along the last dimension, each value on 1 to 256 neighbouring positions
- prefix_x: bfloat16 [4, 512, 1024], P('col', 'row'), may hold values from -6 to 6
- w_qkv: bfloat16 [1024, 3072], P('row', 'col'), may hold values from -1 to 1
- w_out: bfloat16 [1024, 1024], P('row', 'col'), may hold values from -0.1875 to 0.1875
- norm_gain: float32 [1024], replicated, may hold values from 0.1 to 1.9
- norm_bias: float32 [1024], replicated, may hold values from -3 to 3
- page_dest: int32 [4, 8, 64, 1], P('col', 'row'), may hold values from 0 to 7; in each aligned block of 64 rows (0 to 63, 64 to 127, ..., all dimensions but the last counted through in order) at most 16 rows name the same one
Outputs:
- hidden: bfloat16 [4, 8, 512, 1024], P('col', 'row')
- kv_pages: bfloat16 [4, 8, 8, 16, 8, 2048], P('col', 'row')
The draws below stay inside these ranges and needn't reach their ends.
Inputs may be any that keep to these rules, and one draw needn't show every extreme that they name: `page_dest`: no more than 16 pages of one device go to one destination device; some device sends exactly 16 to one destination.
All inputs are finite; a program needn't handle non-finite values.
Results may differ from the reference program's by a relative error of at most 0.0073.
Values may be sent and summed in bfloat16 or wider, within the bound.
A program may use at most 128 MiB of HBM per device.

```python
import math
import jax
import jax.numpy as jnp
import numpy as np
from jax import lax

D = 1024
HEADS = 16
HEAD_DIM = 64
SUF_DEV = 512
REQ_DEV = 4
PAGE = 8
PAGES_DEV = 64
SEG_MOST = 256
MOST = 16
GROUPS = 4
PREFIX = 512
N_ROW = 8


def draw_suffix_x(key, part):
    subkeys = jax.random.split(jax.random.fold_in(key, 11), 4)
    full_shape = (GROUPS, N_ROW, SUF_DEV, D)
    entries = jax.random.normal(subkeys[0], full_shape, jnp.float32)
    half_rows = SUF_DEV // 2
    paired = entries.reshape(GROUPS, N_ROW, half_rows, 2, D)
    leader = paired[:, :, :, 0, :]
    follower = paired[:, :, :, 1, :]
    flagged = jax.random.randint(subkeys[2], (GROUPS, N_ROW, half_rows, 1), 0, 8) == 0
    strength = (3 + jax.random.randint(subkeys[3], (GROUPS, N_ROW, half_rows, 1), 0, 5)).astype(jnp.float32)
    strong_leader = strength * leader
    strong_follower = strength * leader + 0.5 * follower
    leader = jnp.where(flagged, strong_leader, leader)
    follower = jnp.where(flagged, strong_follower, follower)
    joined = jnp.stack([leader, follower], axis=3).reshape(full_shape)
    return jnp.clip(joined, -40.0, 40.0).astype(jnp.bfloat16)


def draw_w_qkv(key, part):
    subkeys = jax.random.split(jax.random.fold_in(key, 23), 1)
    entries = jnp.clip(jax.random.normal(subkeys[0], (3, D, D), jnp.float32), -6.0, 6.0)
    query_part = entries[0]
    key_part = 0.8 * entries[0] + 0.6 * entries[1]
    value_part = entries[2]
    joined = jnp.concatenate([query_part, key_part, value_part], axis=1) * D ** (-0.5)
    return jnp.clip(joined, -1.0, 1.0).astype(jnp.bfloat16)


def block_scale(stream_key, shape, pieces, smallest, largest):
    gain, own = 1.0, jax.random.fold_in(stream_key, 6)
    for position, shards_of in pieces:
        heights = jnp.exp(jax.random.uniform(jax.random.fold_in(own, position), (shards_of,), jnp.float32, smallest / len(pieces), largest / len(pieces)))
        gain = gain * jnp.repeat(heights, shape[position] // shards_of).reshape([-1 if axis == position else 1 for axis in range(len(shape))])
    return gain


def length_profile(count, total, limit, skew):
    portions = [(1 << 20) // math.isqrt(grade ** skew) + 1 for grade in range(2, count + 1)]
    spare, counts = total - limit - (count - 1), [1] * (count - 1)
    while spare > 0:
        movable = [i for i in range(count - 1) if counts[i] < limit]
        whole, remaining = sum([portions[i] for i in movable]), spare
        for i in movable:
            more = min(limit - counts[i], max(1, remaining * portions[i] // whole), spare)
            counts[i] = counts[i] + more
            spare = spare - more
    return np.array([limit] + counts)


def ragged_sizes(rng, count, total, most, skew):
    if count == 2:
        one = jax.random.randint(rng, (), max(1, total - most), min(most, total - 1) + 1)
        return jnp.stack([one, total - one])
    lengths = jnp.asarray(length_profile(count, total, most, skew), jnp.int32)
    twos = (count - 1) // 2
    source_of, sink = lengths[1:1 + 2 * twos:2], lengths[2:2 + 2 * twos:2]
    margin = jnp.minimum(source_of - 1, most - sink)
    passed = jax.random.randint(jax.random.fold_in(rng, 1), (twos,), 0, 1 << 20) % (margin + 1)
    lengths = lengths.at[1:1 + 2 * twos:2].set(source_of - passed).at[2:2 + 2 * twos:2].set(sink + passed)
    return lengths[jax.random.permutation(jax.random.fold_in(rng, 2), count)]


def deal_out(key, own, number, rows, amount, top, reach, lean):
    sequence = jax.random.permutation(key, amount)
    crowded, ordinary = portions_of(amount, rows * top, reach, lean, True), portions_of(amount, rows * top, reach, lean, False)
    places = jnp.arange(amount)

    def named(lengths, rotation):
        used = int((lengths > 0).sum())
        fixed = max(1, used // 4)
        shifted = fixed + (places - fixed + rotation * (used - fixed)) % max(1, amount - fixed)
        return jnp.zeros((amount,), jnp.int32).at[sequence[jnp.where(places < fixed, places, shifted)]].set(jnp.asarray(lengths, jnp.int32))

    lengths = jnp.where(number % 4 == 0, named(crowded, number // 4), named(ordinary, number - number // 4 - 1))
    mixed = jax.random.permutation(jax.random.fold_in(own, 3), amount)
    source_of, receiver = mixed[0:amount // 2 * 2:2], mixed[1:amount // 2 * 2:2]
    room = jnp.minimum(lengths[source_of] - 1, reach - lengths[receiver]) // 2
    room = jnp.where((source_of == sequence[0]) | (receiver == sequence[0]) | (lengths[receiver] == 0), 0, jnp.maximum(room, 0))
    shifted = jax.random.randint(jax.random.fold_in(own, 4), (amount // 2,), 0, 1 << 20) % (room + 1)
    lengths = lengths.at[source_of].add(-shifted).at[receiver].add(shifted)
    members = jnp.searchsorted(jnp.cumsum(lengths), jnp.arange(rows * top), side="right").astype(jnp.int32)
    grid = members.reshape(top, rows).T
    grid = grid[jax.random.permutation(jax.random.fold_in(own, 1), rows)]
    rotation = jax.random.randint(jax.random.fold_in(own, 2), (rows, 1), 0, top)
    return jnp.take_along_axis(grid, (jnp.arange(top)[None, :] + rotation) % top, axis=1)


def portions_of(number_of, total, bound, lean, full):
    weights = [(1 << 20) // math.isqrt(rank ** lean) + 1 for rank in range(1, number_of + 1)]
    largest = bound if full else min(bound, max(-(-total // number_of), total * weights[0] // sum(weights)))
    least = 1 if total - largest >= number_of - 1 else 0
    counts, surplus = [largest] + [least] * (number_of - 1), total - largest - least * (number_of - 1)
    while surplus > 0:
        movable = [i for i in range(1, number_of) if counts[i] < largest] or [i for i in range(1, number_of) if counts[i] < bound]
        whole, remaining = sum([weights[i] for i in movable]), surplus
        for i in movable:
            addition = min(bound - counts[i], max(1, remaining * weights[i] // whole), surplus)
            counts[i] = counts[i] + addition
            surplus = surplus - addition
    return np.array(counts)


def bell_draw(stream_key, shape, width, most, shards=(), kind=jnp.bfloat16):
    values = width * jax.random.normal(stream_key, shape, jnp.float32)
    if shards:
        values = values * block_scale(stream_key, shape, shards, -0.22, 0.18)
    return jnp.clip(values, -most, most).astype(kind)


def setup_inputs(seed: int = 0) -> dict:
    splits = jax.random.split(jax.random.key(seed), 9)
    suffix_x = draw_suffix_x(jax.random.fold_in(splits[8], 71), 0)
    segment_ids = jax.vmap(lambda own: jnp.searchsorted(jnp.cumsum(ragged_sizes(own, REQ_DEV, SUF_DEV, SEG_MOST, 2)), jnp.arange(SUF_DEV), side="right"))(jax.random.split(splits[1], GROUPS * N_ROW)).reshape((GROUPS, N_ROW, SUF_DEV)).astype(jnp.int32)
    prefix_x = bell_draw(splits[2], (GROUPS, PREFIX, D), 1.0, 6.0, ((0, 4), (1, 8)))
    w_qkv = draw_w_qkv(jax.random.fold_in(splits[8], 71), 0)
    w_out = bell_draw(splits[4], (D, D), D ** -0.5, 0.1875, ((0, 8), (1, 4)))
    norm_gain = jnp.clip(1.0 + 0.18 * jax.random.normal(splits[5], (D,), jnp.float32), 0.1, 1.9)
    norm_bias = bell_draw(splits[6], (D,), 0.5, 3.0, (), jnp.float32)
    page_dest_keys = jax.random.split(jax.random.fold_in(splits[7], 1), GROUPS * N_ROW * PAGES_DEV // PAGES_DEV)
    page_dest_turns = jax.random.permutation(jax.random.fold_in(splits[7], 3), GROUPS * N_ROW * PAGES_DEV // PAGES_DEV)
    page_dest = jax.vmap(lambda own, number: deal_out(jax.random.fold_in(splits[7], 2), own, number, PAGES_DEV, N_ROW, 1, MOST, 2))(page_dest_keys, page_dest_turns).reshape((GROUPS, N_ROW, PAGES_DEV, 1))
    return dict(suffix_x=suffix_x, segment_ids=segment_ids, prefix_x=prefix_x, w_qkv=w_qkv, w_out=w_out, norm_gain=norm_gain, norm_bias=norm_bias, page_dest=page_dest)


def layer_norm(mixed, norm_gain, norm_bias):
    center = lax.optimization_barrier(jnp.mean(mixed, axis=-1, keepdims=True))
    spread = lax.optimization_barrier(jnp.mean((mixed - center) ** 2, axis=-1, keepdims=True))
    return ((mixed - center) * lax.rsqrt(spread + 1e-05) * norm_gain + norm_bias).astype(jnp.bfloat16)

def reference(suffix_x, segment_ids, prefix_x, w_qkv, w_out, norm_gain, norm_bias, page_dest):
    w_kv = w_qkv[:, D:]
    factor = HEAD_DIM ** (-0.5)

    def one_group(group):
        states, segments, prefix_states, targets = group
        prefix_kv = jnp.dot(prefix_states, w_kv, preferred_element_type=jnp.float32).astype(jnp.bfloat16)
        key_pre = prefix_kv[:, :D].astype(jnp.float32).reshape(PREFIX, HEADS, HEAD_DIM)
        val_pre = prefix_kv[:, D:].astype(jnp.float32).reshape(PREFIX, HEADS, HEAD_DIM)

        def one_device(item):
            tokens, segment = item
            qkv = jnp.dot(tokens, w_qkv, preferred_element_type=jnp.float32)
            query = (qkv[:, :D] * factor).astype(jnp.bfloat16).astype(jnp.float32).reshape(SUF_DEV, HEADS, HEAD_DIM)
            keyval = qkv[:, D:].astype(jnp.bfloat16)
            key_own = keyval[:, :D].astype(jnp.float32).reshape(SUF_DEV, HEADS, HEAD_DIM)
            val_own = keyval[:, D:].astype(jnp.float32).reshape(SUF_DEV, HEADS, HEAD_DIM)
            score_pre = jnp.einsum('qhd,khd->hqk', query, key_pre)
            score_own = jnp.einsum('qhd,khd->hqk', query, key_own)
            same = segment[:, None] == segment[None, :]
            score_own = jnp.where(same[None], score_own, jnp.float32(-1e+30))
            upper = jnp.maximum(lax.optimization_barrier(jnp.max(score_pre, axis=-1)), lax.optimization_barrier(jnp.max(score_own, axis=-1)))
            exp_pre = jnp.exp(score_pre - upper[..., None])
            exp_own = jnp.exp(score_own - upper[..., None])
            total = lax.optimization_barrier(jnp.sum(exp_pre, axis=-1)) + lax.optimization_barrier(jnp.sum(exp_own, axis=-1))
            accum = jnp.einsum('hqk,khd->hqd', exp_pre.astype(jnp.bfloat16).astype(jnp.float32), val_pre)
            accum = accum + jnp.einsum('hqk,khd->hqd', exp_own.astype(jnp.bfloat16).astype(jnp.float32), val_own)
            attn = (accum / total[..., None]).transpose(1, 0, 2).reshape(SUF_DEV, D).astype(jnp.bfloat16)
            mixed = tokens.astype(jnp.float32) + jnp.dot(attn, w_out, preferred_element_type=jnp.float32)
            return (layer_norm(mixed, norm_gain, norm_bias), keyval)
        hidden, keyval = lax.map(one_device, (states, segments))
        pages = keyval.reshape(N_ROW, PAGES_DEV, PAGE, 2 * D)
        target = targets[:, :, 0].astype(jnp.int32)
        onehot = (target[:, :, None] == jnp.arange(N_ROW, dtype=jnp.int32)[None, None, :]).astype(jnp.int32)
        rank = lax.optimization_barrier(jnp.sum((jnp.cumsum(onehot, axis=1) - onehot) * onehot, axis=2)).astype(jnp.int32)
        source = jnp.broadcast_to(jnp.arange(N_ROW, dtype=jnp.int32)[:, None], (N_ROW, PAGES_DEV))
        placed = jnp.zeros((N_ROW, N_ROW, MOST, PAGE, 2 * D), jnp.bfloat16).at[target, source, rank].set(pages)
        return (hidden, placed)
    hidden, kv_pages = lax.map(one_group, (suffix_x, segment_ids, prefix_x, page_dest))
    return (hidden, kv_pages)
```

```python
import functools

import jax
import jax.numpy as jnp
from jax import lax
from jax.experimental import pallas as pl
from jax.experimental.pallas import tpu as pltpu
from jax.sharding import PartitionSpec as P

HEADS = 16
HEAD_DIM = 64
PAGE = 8
LANES = 128
MESH = pl.DeviceIdType.MESH
BF16 = jnp.bfloat16
F32 = jnp.float32


def spans(col, qc, edge):
    low, high = col * qc, (col + 1) * qc
    cuts = [low] + ([edge] if low < edge < high else []) + [high]
    return list(zip(cuts[:-1], cuts[1:]))


def fused_kernel(dims, wq_ref, wo_ref, px_ref, tok_ref, dest_ref, seg_ref, gain_ref, bias_ref,
                 hid_ref, page_ref, g_s, x_s, q_s, kv_s, attn_s, qm_s, km_s, out_s, in_s,
                 own_sem, w_recv, p_recv, w_z, w_a, w_b, w_s, p_z, p_x, t_send, t_recv):
    nz, nx, ny = dims
    na, nb = nx, ny
    n_row, n_col = nz * nx, ny * 2
    row, col = lax.axis_index("row"), lax.axis_index("col")
    z, x = row // nx, row % nx
    y, core = col // 2, col % 2
    swap = core if nx == ny else core * 0
    rows, qc = wq_ref.shape
    oc = wo_ref.shape[1]
    prow = px_ref.shape[0]
    n_tok, width = tok_ref.shape
    n_pre = n_row * prow
    n_key = n_pre + n_tok
    slab = in_s.shape[1]

    def pick(first, second):
        return first + swap * (second - first)

    ia, ib = pick(x, y), pick(y, x)
    a_peers = [(ia + d) % na for d in range(1, na)]
    b_peers = [(ib + d) % nb for d in range(1, nb)]
    x_peers = [(x + d) % nx for d in range(1, nx)]
    y_peers = [(y + d) % ny for d in range(1, ny)]
    sibling = {"row": row, "col": y * 2 + 1 - core}
    up = {"row": jnp.minimum(z + 1, nz - 1) * nx + x, "col": col}
    down = {"row": jnp.maximum(z - 1, 0) * nx + x, "col": col}

    def name(zb, a, b):
        return pick(b, a) * 2 + core, zb * nx + pick(a, b)

    def device(a, b):
        c, r = name(z, a, b)
        return {"row": r, "col": c}

    def block(c, r):
        return g_s.at[c, pl.ds(pl.multiple_of(r * rows, rows), rows), :]

    def pblock(r):
        return x_s.at[pl.ds(pl.multiple_of(r * prow, prow), prow), :]

    def w_copy(c, r, send, to):
        return pltpu.make_async_remote_copy(
            src_ref=block(c, r), dst_ref=block(c, r), send_sem=send,
            recv_sem=w_recv.at[c, r], device_id=to, device_id_type=MESH)

    def p_copy(r, send, to):
        return pltpu.make_async_remote_copy(
            src_ref=pblock(r), dst_ref=pblock(r), send_sem=send,
            recv_sem=p_recv.at[r], device_id=to, device_id_type=MESH)

    def wait_w(c, r):
        w_copy(c, r, w_s.at[0, 0], sibling).wait_recv()

    def wait_p(r):
        p_copy(r, w_s.at[0, 0], sibling).wait_recv()

    def z_send(zb, direction):
        to = up if direction == 0 else down
        return (w_copy(col, zb * nx + x, w_z.at[direction, zb], to),
                p_copy(zb * nx + x, p_z.at[direction, zb], to))

    def a_send(zb, d):
        c, r = name(zb, ia, ib)
        return w_copy(c, r, w_a.at[d, zb], device(a_peers[d], ib))

    def b_send(zb, a, d):
        c, r = name(zb, a, ib)
        return w_copy(c, r, w_b.at[d, zb, a], device(ia, b_peers[d]))

    def s_send(zb, a, b):
        c, r = name(zb, a, b)
        return w_copy(c, r, w_s.at[c // 2, r], sibling)

    def px_send(zb, d):
        return p_copy(zb * nx + x, p_x.at[d, zb], {"row": z * nx + x_peers[d], "col": col})

    def t_copy(d):
        to = (row + d) % n_row
        return pltpu.make_async_remote_copy(
            src_ref=out_s.at[to], dst_ref=in_s.at[row], send_sem=t_send.at[d],
            recv_sem=t_recv.at[row], device_id={"row": to, "col": col}, device_id_type=MESH)

    def t_wait(src):
        pltpu.make_async_remote_copy(
            src_ref=out_s.at[src], dst_ref=in_s.at[src], send_sem=t_send.at[0],
            recv_sem=t_recv.at[src], device_id=sibling, device_id_type=MESH).wait_recv()

    own = [
        pltpu.make_async_copy(wq_ref, block(col, row).at[:, pl.ds(0, qc)], own_sem.at[0]),
        pltpu.make_async_copy(wo_ref, block(col, row).at[:, pl.ds(qc, oc)], own_sem.at[1]),
        pltpu.make_async_copy(px_ref, pblock(row), own_sem.at[2]),
    ]
    own_tok = pltpu.make_async_copy(tok_ref, x_s.at[pl.ds(n_pre, n_tok), :], own_sem.at[3])
    for copy in own:
        copy.start()
    own_tok.start()

    barrier = pltpu.get_barrier_semaphore()

    def greet(to):
        pl.semaphore_signal(barrier, inc=1, device_id=to, device_id_type=MESH)

    for d in range(1, n_row):
        greet({"row": (row + d) % n_row, "col": col})
    for peer in y_peers:
        greet({"row": row, "col": peer * 2 + core})
    greet(sibling)
    pl.semaphore_wait(barrier, n_row + len(y_peers))
    for copy in own:
        copy.wait()

    def spread(zb, direction):
        if direction in (0, None):
            @pl.when(z < nz - 1)
            def _():
                for copy in z_send(zb, 0):
                    copy.start()
        if direction in (1, None):
            @pl.when(z > 0)
            def _():
                for copy in z_send(zb, 1):
                    copy.start()
        for d in range(na - 1):
            a_send(zb, d).start()
        for d in range(nb - 1):
            b_send(zb, ia, d).start()
        for d in range(nx - 1):
            px_send(zb, d).start()
        s_send(zb, ia, ib).start()

    def from_a(zb):
        for peer in a_peers:
            wait_w(*name(zb, peer, ib))
            for d in range(nb - 1):
                b_send(zb, peer, d).start()
            s_send(zb, peer, ib).start()

    def at_distance(step, action):
        if step == 0:
            action(z, None)
            return

        @pl.when(z >= step)
        def _():
            action(z - step, 0)

        @pl.when(z + step < nz)
        def _():
            action(z + step, 1)

    def arrived(zb, direction):
        if direction is not None:
            wait_w(col, zb * nx + x)
            wait_p(zb * nx + x)
        spread(zb, direction)

    at_distance(0, arrived)

    own_tok.wait()
    tokens = x_s.at[pl.ds(n_pre, n_tok), :]

    n_page = dest_ref.shape[1]
    most = slab // PAGE
    target = dest_ref[...].astype(F32)
    along = jnp.broadcast_to(target, (LANES, n_page)).T[:, :1]
    first_page = lax.broadcasted_iota(jnp.int32, (n_page, n_page), 0)
    second_page = lax.broadcasted_iota(jnp.int32, (n_page, n_page), 1)
    earlier = jnp.where((along == target) & (first_page < second_page), 1.0, 0.0)
    slot = target * most + jnp.sum(earlier, axis=0, keepdims=True)
    page_of = lax.broadcasted_iota(jnp.int32, (n_page, n_tok), 1) // PAGE
    member = jnp.where(page_of == lax.broadcasted_iota(jnp.int32, (n_page, n_tok), 0), 1.0, 0.0)
    slot_of = jnp.dot(jnp.broadcast_to(slot, (8, n_page)), member, precision=lax.Precision.HIGHEST,
                      preferred_element_type=F32)[:1]
    inside = lax.broadcasted_iota(jnp.int32, (1, n_tok), 1) % PAGE
    place = slot_of * PAGE + inside.astype(F32)

    def fill(i, _):
        first = i * slab
        want = lax.broadcasted_iota(jnp.int32, (slab, n_tok), 0) + first
        chosen = jnp.where(want.astype(F32) == place, 1.0, 0.0).astype(BF16)
        out_s[i] = jnp.dot(chosen, tokens[...], preferred_element_type=F32).astype(BF16)
        return 0

    lax.fori_loop(0, n_row, fill, 0)
    in_s[row] = out_s[row]

    for step in range(1, nz):
        at_distance(step, arrived)
        at_distance(step - 1, lambda zb, _: from_a(zb))
    for d in range(nx, n_row, nx):
        t_copy(d).start()
    at_distance(nz - 1, lambda zb, _: from_a(zb))

    lane = lax.broadcasted_iota(jnp.int32, (n_tok, LANES), 1)
    low_half = lane < HEAD_DIM
    segment = jnp.broadcast_to(seg_ref[...].astype(F32), (LANES, n_tok)).T
    match = jnp.where(low_half, lane, lane - HEAD_DIM).astype(F32) == segment
    for half in range(2):
        part = low_half if half == 0 else jnp.logical_not(low_half)
        qm_s[half] = jnp.where(match, 0.0, jnp.where(part, -1e30, 0.0)).astype(BF16)
        km_s[half, n_pre:n_key, :] = jnp.where(match & part, 1.0, 0.0).astype(BF16)
        km_s[half, 0:n_pre, :] = jnp.zeros((n_pre, LANES), BF16)

    def later(step):
        def take(zb, _):
            for a in [ia] + a_peers:
                for peer in b_peers:
                    wait_w(*name(zb, a, peer))
                    s_send(zb, a, peer).start()
        at_distance(step, take)

    for step in range(nz):
        later(step)
    for zb in range(nz):
        for peer in x_peers:
            wait_p(zb * nx + peer)
    for yb in range(ny):
        for r in range(n_row):
            wait_w(yb * 2 + 1 - core, r)

    for d in range(1, n_row):
        if d % nx:
            t_copy(d).start()

    for c in range(n_col):
        for low, high in spans(c, qc, width):
            w = g_s[c, :, low - c * qc:high - c * qc]
            if high <= width:
                q_s[:, low:high] = (jnp.dot(tokens[...], w, preferred_element_type=F32)
                                    * HEAD_DIM ** (-0.5)).astype(BF16)
            else:
                kv_s[:, low - width:high - width] = jnp.dot(
                    x_s[...], w, preferred_element_type=F32).astype(BF16)
    lane_row = lax.broadcasted_iota(jnp.int32, (1, LANES), 1)
    keep = [jnp.where(lane_row < HEAD_DIM, 1.0, 0.0).astype(BF16),
            jnp.where(lane_row < HEAD_DIM, 0.0, 1.0).astype(BF16)]
    tile = min(256, n_tok)

    def pair(j, _):
        cols = pl.ds(pl.multiple_of(j * LANES, LANES), LANES)
        vcols = pl.ds(pl.multiple_of(width + j * LANES, LANES), LANES)
        keys = kv_s[:, cols]
        values = kv_s[:, vcols]
        k_aug = [keys * keep[h] + km_s[1 - h] for h in range(2)]
        v_aug = [values * keep[h] + keep[1 - h] for h in range(2)]
        for t in range(n_tok // tile):
            span = slice(t * tile, (t + 1) * tile)
            q = q_s[span, cols]
            outs = []
            for h in range(2):
                q_aug = q * keep[h] + qm_s[1 - h, span, :]
                s = lax.dot_general(q_aug, k_aug[h], (((1,), (1,)), ((), ())),
                                    preferred_element_type=F32)
                m = jnp.max(s, axis=-1, keepdims=True)
                p = jnp.exp(s - m).astype(BF16)
                outs.append(jnp.dot(p, v_aug[h], preferred_element_type=F32))
            first = lax.broadcasted_iota(jnp.int32, (tile, LANES), 1) < HEAD_DIM
            num = jnp.where(first, outs[0], outs[1])
            total = pltpu.roll(jnp.where(first, outs[1], outs[0]), HEAD_DIM, 1)
            attn_s[span, cols] = (num / total).astype(BF16)
        return 0

    lax.fori_loop(0, width // LANES, pair, 0)
    for t in range(n_tok // tile):
        span = slice(t * tile, (t + 1) * tile)
        a = attn_s[span, :]
        mixed = tokens[span, :].astype(F32) + jnp.concatenate(
            [jnp.dot(a, g_s[c, :, qc:qc + oc], preferred_element_type=F32) for c in range(n_col)],
            axis=1)
        center = jnp.mean(mixed, axis=-1, keepdims=True)
        off = mixed - center
        spread_of = jnp.mean(off * off, axis=-1, keepdims=True)
        hid_ref[span, :] = (off * lax.rsqrt(spread_of + 1e-05) * gain_ref[...] + bias_ref[...]).astype(BF16)

    group = max(1, min(n_row, 256 // slab))

    for i in range(n_row // group):
        for src in range(i * group, (i + 1) * group):
            @pl.when(row != src)
            def _():
                t_wait(src)
        some = in_s[i * group:(i + 1) * group].reshape(group * slab, width)
        for c in range(n_col):
            for low, high in spans(c, qc, width):
                if low >= width:
                    page_ref[i * group:(i + 1) * group, :, low - width:high - width] = jnp.dot(
                        some, g_s[c, :, low - c * qc:high - c * qc],
                        preferred_element_type=F32).astype(BF16).reshape(group, slab, high - low)

    for zb in range(nz):
        @pl.when((z < nz - 1) & (zb <= z))
        def _():
            for copy in z_send(zb, 0):
                copy.wait_send()

        @pl.when((z > 0) & (zb >= z))
        def _():
            for copy in z_send(zb, 1):
                copy.wait_send()

        for d in range(na - 1):
            a_send(zb, d).wait_send()
        for d in range(nx - 1):
            px_send(zb, d).wait_send()
        for a in range(na):
            for d in range(nb - 1):
                b_send(zb, a, d).wait_send()
            for b in range(nb):
                s_send(zb, a, b).wait_send()
    for d in range(1, n_row):
        t_copy(d).wait_send()


def fused(dims, w_qkv, w_out, prefix, tokens, dest, segment, gain, bias, slab):
    nz, nx, ny = dims
    n_row, n_col = nz * nx, ny * 2
    rows, qc = w_qkv.shape
    oc = w_out.shape[1]
    prow, width = prefix.shape
    n_tok = tokens.shape[0]
    n_pre = n_row * prow
    n_key = n_pre + n_tok
    dma = pltpu.SemaphoreType.DMA
    anywhere = pl.BlockSpec(memory_space=pl.ANY)
    vmem = pl.BlockSpec(memory_space=pltpu.VMEM)
    return pl.pallas_call(
        functools.partial(fused_kernel, dims),
        out_shape=(pltpu.VMEM((n_tok, width), BF16),
                   pltpu.VMEM((n_row, slab, 2 * width), BF16)),
        in_specs=[anywhere] * 4 + [vmem] * 4,
        out_specs=(vmem, vmem),
        scratch_shapes=[
            pltpu.VMEM((n_col, n_row * rows, qc + oc), BF16),
            pltpu.VMEM((n_key, width), BF16),
            pltpu.VMEM((n_tok, width), BF16),
            pltpu.VMEM((n_key, 2 * width), BF16),
            pltpu.VMEM((n_tok, width), BF16),
            pltpu.VMEM((2, n_tok, LANES), BF16),
            pltpu.VMEM((2, n_key, LANES), BF16),
            pltpu.VMEM((n_row, slab, width), BF16),
            pltpu.VMEM((n_row, slab, width), BF16),
            dma((4,)), dma((n_col, n_row)), dma((n_row,)), dma((2, nz)),
            dma((max(1, nx - 1), nz)), dma((max(1, ny - 1), nz, nx)), dma((ny, n_row)),
            dma((2, nz)), dma((max(1, nx - 1), nz)), dma((n_row,)), dma((n_row,))],
        compiler_params=pltpu.CompilerParams(
            collective_id=0, has_side_effects=True, vmem_limit_bytes=54 * 1024 * 1024),
        name="fused",
    )(w_qkv, w_out, prefix, tokens, dest, segment, gain, bias)


def settle_kernel(parts, hid_ref, page_ref, hid_out, page_out, sem):
    n = page_ref.shape[0]
    step = n // parts
    copies = [pltpu.make_async_copy(page_ref.at[pl.ds(i * step, step)], page_out.at[pl.ds(i * step, step)], sem.at[i])
              for i in range(parts)]
    copies.append(pltpu.make_async_copy(hid_ref, hid_out, sem.at[parts]))
    for copy in copies:
        copy.start()
    for copy in copies:
        copy.wait()


def settle(hidden, pages):
    anywhere = pl.BlockSpec(memory_space=pl.ANY)
    parts = min(8, pages.shape[0])
    return pl.pallas_call(
        functools.partial(settle_kernel, parts),
        out_shape=(jax.ShapeDtypeStruct(hidden.shape, BF16), jax.ShapeDtypeStruct(pages.shape, BF16)),
        in_specs=[anywhere] * 2,
        out_specs=(pl.BlockSpec(memory_space=pltpu.HBM),) * 2,
        scratch_shapes=[pltpu.SemaphoreType.DMA((parts + 1,))],
        compiler_params=pltpu.CompilerParams(vmem_limit_bytes=1024 * 1024),
        name="settle",
    )(hidden, pages)


def local(dims, suffix_x, segment_ids, prefix_x, w_qkv, w_out, norm_gain, norm_bias, page_dest):
    width = suffix_x.shape[-1]
    tokens = suffix_x[0, 0]
    n_tok = tokens.shape[0]
    ranks = lax.axis_size("row")
    pages_dev = n_tok // PAGE
    most = max(2, 2 * pages_dev // ranks)
    hidden, pages = fused(dims, w_qkv, w_out, prefix_x[0], tokens, page_dest[0, 0].reshape(1, pages_dev),
                          segment_ids[0], norm_gain[None], norm_bias[None], most * PAGE)
    hidden, pages = settle(hidden, pages)
    pages = pages.reshape(ranks, most, PAGE, 2 * width)
    return (hidden[None, None], pages[None, None])


def solution(mesh):
    n_row, n_col = mesh.shape["row"], mesh.shape["col"]
    ny = n_col // 2
    nx = ny if n_row % ny == 0 else 1
    dims = (n_row // nx, nx, ny)
    in_specs = (
        P("col", "row", None, None),
        P("col", "row", None),
        P("col", "row", None),
        P("row", "col"),
        P("row", "col"),
        P(),
        P(),
        P("col", "row", None, None),
    )
    out_specs = (P("col", "row", None, None), P("col", "row", None, None, None, None))
    return jax.shard_map(functools.partial(local, dims), mesh=mesh, in_specs=in_specs,
                         out_specs=out_specs, check_vma=False)
```

```python
import functools

import jax
import jax.numpy as jnp
from jax import lax
from jax.experimental import pallas as pl
from jax.experimental.pallas import tpu as pltpu
from jax.sharding import PartitionSpec as P

HEADS = 16
HEAD_DIM = 64
PAGE = 8
LANES = 128
MESH = pl.DeviceIdType.MESH
BF16 = jnp.bfloat16
F32 = jnp.float32


def spans(col, qc, edge):
    low, high = col * qc, (col + 1) * qc
    cuts = [low] + ([edge] if low < edge < high else []) + [high]
    return list(zip(cuts[:-1], cuts[1:]))


def fused_kernel(dims, wq_ref, wo_ref, px_ref, tok_ref, dest_ref, seg_ref, gain_ref, bias_ref,
                 hid_ref, page_ref, gq_s, go_s, x_s, q_s, kv_s, attn_s, qm_s, km_s, out_s, in_s,
                 own_sem, w_recv, p_recv, oz_recv, o_recv, os_recv, w_z, w_x, w_y, w_xy, w_yx, w_s,
                 p_z, p_x, o_z, o_x, o_y, o_xy, o_s, t_send, t_recv):
    nz, nx, ny = dims
    n_row, n_col = nz * nx, ny * 2
    row, col = lax.axis_index("row"), lax.axis_index("col")
    z, x = row // nx, row % nx
    y, core = col // 2, col % 2
    rows, qc = wq_ref.shape
    oc = wo_ref.shape[1]
    prow = px_ref.shape[0]
    n_tok, width = tok_ref.shape
    n_pre = n_row * prow
    n_key = n_pre + n_tok
    slab = in_s.shape[1]
    cut = max(16, rows // 64 * 16)

    x_peers = [(x + d) % nx for d in range(1, nx)]
    y_peers = [(y + d) % ny for d in range(1, ny)]
    sibling = {"row": row, "col": y * 2 + 1 - core}
    up = {"row": jnp.minimum(z + 1, nz - 1) * nx + x, "col": col}
    down = {"row": jnp.maximum(z - 1, 0) * nx + x, "col": col}

    def to_x(d):
        return {"row": z * nx + x_peers[d], "col": col}

    def to_y(d):
        return {"row": row, "col": y_peers[d] * 2 + core}

    def remote(ref, send, recv, to):
        return pltpu.make_async_remote_copy(
            src_ref=ref, dst_ref=ref, send_sem=send, recv_sem=recv, device_id=to, device_id_type=MESH)

    def wblock(b, zb, a, part=None, side=None):
        c, r = b * 2 + (core if side is None else side), zb * nx + a
        first, count = {None: (0, rows), 0: (0, cut), 1: (cut, rows - cut)}[part]
        return gq_s.at[c, pl.ds(pl.multiple_of(r * rows + first, 16), count), :], w_recv.at[c, r]

    def w_copy(b, zb, a, send, to, part=None, side=None):
        ref, recv = wblock(b, zb, a, part, side)
        return remote(ref, send, recv, to)

    def wait_w(b, zb, a, side=None):
        w_copy(b, zb, a, w_s.at[0, 0], sibling, None, side).wait_recv()

    def x_send(zb, d):
        return w_copy(y, zb, x, w_x.at[d, zb], to_x(d))

    def y_send(zb, d):
        return w_copy(y, zb, x, w_y.at[d, zb], to_y(d))

    def xy_send(zb, i, d):
        return w_copy(y, zb, x_peers[i], w_xy.at[i, d, zb], to_y(d), 1)

    def yx_send(zb, j, d):
        return w_copy(y_peers[j], zb, x, w_yx.at[j, d, zb], to_x(d), 0)

    def s_send(b, zb, a):
        return w_copy(b, zb, a, w_s.at[b, zb * nx + a], sibling)

    def wz_send(zb, direction):
        return w_copy(y, zb, x, w_z.at[direction, zb], up if direction == 0 else down)

    def pblock(r):
        return x_s.at[pl.ds(pl.multiple_of(r * prow, prow), prow), :]

    def p_copy(r, send, to):
        return remote(pblock(r), send, p_recv.at[r], to)

    def wait_p(r):
        p_copy(r, w_s.at[0, 0], sibling).wait_recv()

    def pz_send(zb, direction):
        return p_copy(zb * nx + x, p_z.at[direction, zb], up if direction == 0 else down)

    def px_send(zb, d):
        return p_copy(zb * nx + x, p_x.at[d, zb], to_x(d))

    def oz_send(zb, direction):
        ref = go_s.at[col, zb, pl.ds(pl.multiple_of(x * rows, 16), rows), :]
        return remote(ref, o_z.at[direction, zb], oz_recv.at[zb], up if direction == 0 else down)

    def o_plane(b, a, side):
        return go_s.at[b * 2 + side, :, pl.ds(pl.multiple_of(a * rows, 16), rows), :]

    def o_copy(b, a, send, to):
        return remote(o_plane(b, a, core), send, o_recv.at[b, a], to)

    def ox_send(d):
        return o_copy(y, x, o_x.at[d], to_x(d))

    def oy_send(d):
        return o_copy(y, x, o_y.at[d], to_y(d))

    def oxy_send(i, d):
        return o_copy(y, x_peers[i], o_xy.at[i, d], to_y(d))

    def os_send(b, a):
        return remote(o_plane(b, a, core), o_s.at[b, a], os_recv.at[b, a], sibling)

    def wait_o(b, a):
        o_copy(b, a, o_s.at[0, 0], sibling).wait_recv()

    def wait_os(b, a):
        remote(o_plane(b, a, 1 - core), o_s.at[0, 0], os_recv.at[b, a], sibling).wait_recv()

    paired = nz & (nz - 1) == 0 and nx & (nx - 1) == 0
    offsets = [(dz, dx) for dx in range(nx) for dz in [0] + list(range(nz - 1, 0, -1))]

    def partner(k, sign):
        dz, dx = offsets[k]
        if paired:
            return (z ^ dz) * nx + (x ^ dx)
        return (z + sign * dz + nz) % nz * nx + (x + sign * dx + nx) % nx

    def t_copy(k):
        to = partner(k, 1)
        return pltpu.make_async_remote_copy(
            src_ref=out_s.at[to], dst_ref=in_s.at[k], send_sem=t_send.at[k],
            recv_sem=t_recv.at[k], device_id={"row": to, "col": col}, device_id_type=MESH)

    own = [
        pltpu.make_async_copy(wq_ref, wblock(y, z, x)[0], own_sem.at[0]),
        pltpu.make_async_copy(wo_ref, go_s.at[col, z, pl.ds(pl.multiple_of(x * rows, 16), rows), :],
                              own_sem.at[1]),
        pltpu.make_async_copy(px_ref, pblock(row), own_sem.at[2]),
    ]
    own_tok = pltpu.make_async_copy(tok_ref, x_s.at[pl.ds(n_pre, n_tok), :], own_sem.at[3])
    for copy in own:
        copy.start()
    own_tok.start()

    barrier = pltpu.get_barrier_semaphore()

    def greet(to):
        pl.semaphore_signal(barrier, inc=1, device_id=to, device_id_type=MESH)

    for d in range(1, n_row):
        greet({"row": (row + d) % n_row, "col": col})
    for d in range(ny - 1):
        greet(to_y(d))
    greet(sibling)
    pl.semaphore_wait(barrier, n_row + ny - 1)
    for copy in own:
        copy.wait()

    def at_distance(step, action):
        if step < 0 or step >= nz:
            return
        if step == 0:
            action(z, None)
            return

        @pl.when(z >= step)
        def _():
            action(z - step, 0)

        @pl.when(z + step < nz)
        def _():
            action(z + step, 1)

    def forward(send, zb, direction):
        if direction in (0, None):
            @pl.when(z < nz - 1)
            def _():
                send(zb, 0).start()
        if direction in (1, None):
            @pl.when(z > 0)
            def _():
                send(zb, 1).start()

    def from_z(zb, direction):
        if direction is not None:
            wait_w(y, zb, x)
        forward(wz_send, zb, direction)
        for d in range(nx - 1):
            x_send(zb, d).start()
        for d in range(ny - 1):
            y_send(zb, d).start()
        s_send(y, zb, x).start()

    def from_xy(zb, _):
        for i, a in enumerate(x_peers):
            wait_w(y, zb, a)
            for d in range(ny - 1):
                xy_send(zb, i, d).start()
            s_send(y, zb, a).start()
        for j, b in enumerate(y_peers):
            wait_w(b, zb, x)
            for d in range(nx - 1):
                yx_send(zb, j, d).start()
            s_send(b, zb, x).start()

    def from_diagonal(zb, _):
        for b in y_peers:
            for a in x_peers:
                wait_w(b, zb, a)
                s_send(b, zb, a).start()

    def prefix_from_z(zb, direction):
        if direction is not None:
            wait_p(zb * nx + x)
        forward(pz_send, zb, direction)
        for d in range(nx - 1):
            px_send(zb, d).start()

    def out_from_z(zb, direction):
        if direction is None:
            forward(oz_send, zb, direction)
            return

        @pl.when((z < nz - 1) if direction == 0 else (z > 0))
        def _():
            oz_send(zb, direction).wait_recv()
            oz_send(zb, direction).start()

    def out_rest(zb, direction):
        if direction is not None:
            @pl.when((z == nz - 1) if direction == 0 else (z == 0))
            def _():
                oz_send(zb, direction).wait_recv()

    at_distance(0, from_z)

    own_tok.wait()
    tokens = x_s.at[pl.ds(n_pre, n_tok), :]

    n_page = dest_ref.shape[1]
    most = slab // PAGE
    target = dest_ref[...].astype(F32)
    along = jnp.broadcast_to(target, (LANES, n_page)).T[:, :1]
    first_page = lax.broadcasted_iota(jnp.int32, (n_page, n_page), 0)
    second_page = lax.broadcasted_iota(jnp.int32, (n_page, n_page), 1)
    earlier = jnp.where((along == target) & (first_page < second_page), 1.0, 0.0)
    slot = target * most + jnp.sum(earlier, axis=0, keepdims=True)
    page_of = lax.broadcasted_iota(jnp.int32, (n_page, n_tok), 1) // PAGE
    member = jnp.where(page_of == lax.broadcasted_iota(jnp.int32, (n_page, n_tok), 0), 1.0, 0.0)
    slot_of = jnp.dot(jnp.broadcast_to(slot, (8, n_page)), member, precision=lax.Precision.HIGHEST,
                      preferred_element_type=F32)[:1]
    inside = lax.broadcasted_iota(jnp.int32, (1, n_tok), 1) % PAGE
    place = slot_of * PAGE + inside.astype(F32)

    def fill(i, _):
        first = i * slab
        want = lax.broadcasted_iota(jnp.int32, (slab, n_tok), 0) + first
        chosen = jnp.where(want.astype(F32) == place, 1.0, 0.0).astype(BF16)
        out_s[i] = jnp.dot(chosen, tokens[...], preferred_element_type=F32).astype(BF16)
        return 0

    lax.fori_loop(0, n_row, fill, 0)
    in_s[0] = out_s[row]

    for step in range(1, nz):
        at_distance(step, from_z)
        at_distance(step - 1, prefix_from_z)
        at_distance(step - 1, out_from_z)
    at_distance(0, from_xy)
    at_distance(1, from_xy)
    at_distance(nz - 1, prefix_from_z)
    at_distance(nz - 1, out_from_z)
    for step in range(2, nz):
        at_distance(step, from_xy)
    for k in range(1, nz):
        t_copy(k).start()
    for step in range(1, nz):
        at_distance(step, out_rest)
    for d in range(nx - 1):
        ox_send(d).start()
    os_send(y, x).start()

    lane = lax.broadcasted_iota(jnp.int32, (n_tok, LANES), 1)
    low_half = lane < HEAD_DIM
    segment = jnp.broadcast_to(seg_ref[...].astype(F32), (LANES, n_tok)).T
    match = jnp.where(low_half, lane, lane - HEAD_DIM).astype(F32) == segment
    for half in range(2):
        part = low_half if half == 0 else jnp.logical_not(low_half)
        qm_s[half] = jnp.where(match, 0.0, jnp.where(part, -1e30, 0.0)).astype(BF16)
        km_s[half, n_pre:n_key, :] = jnp.where(match & part, 1.0, 0.0).astype(BF16)
        km_s[half, 0:n_pre, :] = jnp.zeros((n_pre, LANES), BF16)

    for zb in range(nz):
        for a in x_peers:
            wait_p(zb * nx + a)
    for zb in range(nz):
        for a in range(nx):
            wait_w(y, zb, a, 1 - core)

    low_of = []
    for c in range(n_col):
        low_of.append(spans(c, qc, width))

    def project(c):
        for low, high in low_of[c]:
            w = gq_s[c, :, low - c * qc:high - c * qc]
            if high <= width:
                q_s[:, low:high] = (jnp.dot(tokens[...], w, preferred_element_type=F32)
                                    * HEAD_DIM ** (-0.5)).astype(BF16)
            else:
                kv_s[:, low - width:high - width] = jnp.dot(
                    x_s[...], w, preferred_element_type=F32).astype(BF16)

    def project_side(b):
        for side in range(2):
            project(b * 2 + side)

    for b in range(ny):
        @pl.when(y == b)
        def _():
            project_side(b)

    for step in range(nz):
        at_distance(step, from_diagonal)
    for b in y_peers:
        for zb in range(nz):
            for a in range(nx):
                wait_w(b, zb, a, 1 - core)
    for d in range(ny - 1):
        oy_send(d).start()
    for k in range(nz, n_row):
        t_copy(k).start()

    for b in range(ny):
        @pl.when(y != b)
        def _():
            project_side(b)

    lane_row = lax.broadcasted_iota(jnp.int32, (1, LANES), 1)
    keep = [jnp.where(lane_row < HEAD_DIM, 1.0, 0.0).astype(BF16),
            jnp.where(lane_row < HEAD_DIM, 0.0, 1.0).astype(BF16)]
    tile = min(256, n_tok)

    def pair(j, _):
        @pl.when(j == 1)
        def _():
            for i, a in enumerate(x_peers):
                wait_o(y, a)
                for d in range(ny - 1):
                    oxy_send(i, d).start()
                os_send(y, a).start()

        @pl.when(j == 3)
        def _():
            for b in y_peers:
                wait_o(b, x)
                os_send(b, x).start()

        @pl.when(j == 5)
        def _():
            for b in y_peers:
                for a in x_peers:
                    wait_o(b, a)
                    os_send(b, a).start()

        cols = pl.ds(pl.multiple_of(j * LANES, LANES), LANES)
        vcols = pl.ds(pl.multiple_of(width + j * LANES, LANES), LANES)
        keys = kv_s[:, cols]
        values = kv_s[:, vcols]
        k_aug = [keys * keep[h] + km_s[1 - h] for h in range(2)]
        v_aug = [values * keep[h] + keep[1 - h] for h in range(2)]
        for t in range(n_tok // tile):
            span = slice(t * tile, (t + 1) * tile)
            q = q_s[span, cols]
            outs = []
            for h in range(2):
                q_aug = q * keep[h] + qm_s[1 - h, span, :]
                s = lax.dot_general(q_aug, k_aug[h], (((1,), (1,)), ((), ())),
                                    preferred_element_type=F32)
                m = jnp.max(s, axis=-1, keepdims=True)
                p = jnp.exp(s - m).astype(BF16)
                outs.append(jnp.dot(p, v_aug[h], preferred_element_type=F32))
            first = lax.broadcasted_iota(jnp.int32, (tile, LANES), 1) < HEAD_DIM
            num = jnp.where(first, outs[0], outs[1])
            total = pltpu.roll(jnp.where(first, outs[1], outs[0]), HEAD_DIM, 1)
            attn_s[span, cols] = (num / total).astype(BF16)
        return 0

    lax.fori_loop(0, width // LANES, pair, 0)

    for b in range(ny):
        for a in range(nx):
            wait_os(b, a)
    for t in range(n_tok // tile):
        span = slice(t * tile, (t + 1) * tile)
        a = attn_s[span, :]
        mixed = tokens[span, :].astype(F32) + jnp.concatenate(
            [jnp.dot(a, go_s[c].reshape(n_row * rows, oc), preferred_element_type=F32)
             for c in range(n_col)], axis=1)
        center = jnp.mean(mixed, axis=-1, keepdims=True)
        off = mixed - center
        spread_of = jnp.mean(off * off, axis=-1, keepdims=True)
        hid_ref[span, :] = (off * lax.rsqrt(spread_of + 1e-05) * gain_ref[...] + bias_ref[...]).astype(BF16)

    group = max(1, min(n_row, 256 // slab))

    for i in range(n_row // group):
        members = range(i * group, (i + 1) * group)
        for k in members:
            if k:
                t_copy(k).wait_recv()
        some = in_s[i * group:(i + 1) * group].reshape(group * slab, width)
        for c in range(n_col):
            for low, high in low_of[c]:
                if low >= width:
                    made = jnp.dot(some, gq_s[c, :, low - c * qc:high - c * qc],
                                   preferred_element_type=F32).astype(BF16)
                    for j, k in enumerate(members):
                        page_ref[partner(k, -1), :, low - width:high - width] = made[j * slab:(j + 1) * slab]

    for zb in range(nz):
        @pl.when((z < nz - 1) & (zb <= z))
        def _():
            for send in (wz_send, pz_send, oz_send):
                send(zb, 0).wait_send()

        @pl.when((z > 0) & (zb >= z))
        def _():
            for send in (wz_send, pz_send, oz_send):
                send(zb, 1).wait_send()

        for d in range(nx - 1):
            x_send(zb, d).wait_send()
            px_send(zb, d).wait_send()
            for j in range(ny - 1):
                yx_send(zb, j, d).wait_send()
        for d in range(ny - 1):
            y_send(zb, d).wait_send()
            for i in range(nx - 1):
                xy_send(zb, i, d).wait_send()
        for b in range(ny):
            for a in range(nx):
                s_send(b, zb, a).wait_send()
    for d in range(nx - 1):
        ox_send(d).wait_send()
    for d in range(ny - 1):
        oy_send(d).wait_send()
        for i in range(nx - 1):
            oxy_send(i, d).wait_send()
    for b in range(ny):
        for a in range(nx):
            os_send(b, a).wait_send()
    for k in range(1, n_row):
        t_copy(k).wait_send()


def fused(dims, w_qkv, w_out, prefix, tokens, dest, segment, gain, bias, slab):
    nz, nx, ny = dims
    n_row, n_col = nz * nx, ny * 2
    rows, qc = w_qkv.shape
    oc = w_out.shape[1]
    prow, width = prefix.shape
    n_tok = tokens.shape[0]
    n_pre = n_row * prow
    n_key = n_pre + n_tok
    dma = pltpu.SemaphoreType.DMA
    anywhere = pl.BlockSpec(memory_space=pl.ANY)
    vmem = pl.BlockSpec(memory_space=pltpu.VMEM)
    xs, ys = max(1, nx - 1), max(1, ny - 1)
    return pl.pallas_call(
        functools.partial(fused_kernel, dims),
        out_shape=(pltpu.VMEM((n_tok, width), BF16),
                   pltpu.VMEM((n_row, slab, 2 * width), BF16)),
        in_specs=[anywhere] * 4 + [vmem] * 4,
        out_specs=(vmem, vmem),
        scratch_shapes=[
            pltpu.VMEM((n_col, n_row * rows, qc), BF16),
            pltpu.VMEM((n_col, nz, nx * rows, oc), BF16),
            pltpu.VMEM((n_key, width), BF16),
            pltpu.VMEM((n_tok, width), BF16),
            pltpu.VMEM((n_key, 2 * width), BF16),
            pltpu.VMEM((n_tok, width), BF16),
            pltpu.VMEM((2, n_tok, LANES), BF16),
            pltpu.VMEM((2, n_key, LANES), BF16),
            pltpu.VMEM((n_row, slab, width), BF16),
            pltpu.VMEM((n_row, slab, width), BF16),
            dma((4,)), dma((n_col, n_row)), dma((n_row,)), dma((nz,)), dma((ny, nx)), dma((ny, nx)),
            dma((2, nz)), dma((xs, nz)), dma((ys, nz)), dma((xs, ys, nz)), dma((ys, xs, nz)), dma((ny, n_row)),
            dma((2, nz)), dma((xs, nz)), dma((2, nz)), dma((xs,)), dma((ys,)), dma((xs, ys)), dma((ny, nx)),
            dma((n_row,)), dma((n_row,))],
        compiler_params=pltpu.CompilerParams(
            collective_id=0, has_side_effects=True, vmem_limit_bytes=54 * 1024 * 1024),
        name="fused",
    )(w_qkv, w_out, prefix, tokens, dest, segment, gain, bias)


def settle_kernel(parts, hid_ref, page_ref, hid_out, page_out, sem):
    n = page_ref.shape[0]
    step = n // parts
    copies = [pltpu.make_async_copy(page_ref.at[pl.ds(i * step, step)], page_out.at[pl.ds(i * step, step)], sem.at[i])
              for i in range(parts)]
    copies.append(pltpu.make_async_copy(hid_ref, hid_out, sem.at[parts]))
    for copy in copies:
        copy.start()
    for copy in copies:
        copy.wait()


def settle(hidden, pages):
    anywhere = pl.BlockSpec(memory_space=pl.ANY)
    parts = min(8, pages.shape[0])
    return pl.pallas_call(
        functools.partial(settle_kernel, parts),
        out_shape=(jax.ShapeDtypeStruct(hidden.shape, BF16), jax.ShapeDtypeStruct(pages.shape, BF16)),
        in_specs=[anywhere] * 2,
        out_specs=(pl.BlockSpec(memory_space=pltpu.HBM),) * 2,
        scratch_shapes=[pltpu.SemaphoreType.DMA((parts + 1,))],
        compiler_params=pltpu.CompilerParams(vmem_limit_bytes=1024 * 1024),
        name="settle",
    )(hidden, pages)


def local(dims, suffix_x, segment_ids, prefix_x, w_qkv, w_out, norm_gain, norm_bias, page_dest):
    width = suffix_x.shape[-1]
    tokens = suffix_x[0, 0]
    n_tok = tokens.shape[0]
    ranks = lax.axis_size("row")
    pages_dev = n_tok // PAGE
    most = max(2, 2 * pages_dev // ranks)
    hidden, pages = fused(dims, w_qkv, w_out, prefix_x[0], tokens, page_dest[0, 0].reshape(1, pages_dev),
                          segment_ids[0], norm_gain[None], norm_bias[None], most * PAGE)
    hidden, pages = settle(hidden, pages)
    pages = pages.reshape(ranks, most, PAGE, 2 * width)
    return (hidden[None, None], pages[None, None])


def solution(mesh):
    n_row, n_col = mesh.shape["row"], mesh.shape["col"]
    ny = n_col // 2
    nx = ny if n_row % ny == 0 else 1
    dims = (n_row // nx, nx, ny)
    in_specs = (
        P("col", "row", None, None),
        P("col", "row", None),
        P("col", "row", None),
        P("row", "col"),
        P("row", "col"),
        P(),
        P(),
        P("col", "row", None, None),
    )
    out_specs = (P("col", "row", None, None), P("col", "row", None, None, None, None))
    return jax.shard_map(functools.partial(local, dims), mesh=mesh, in_specs=in_specs,
                         out_specs=out_specs, check_vma=False)
```

```python
import functools

import jax
import jax.numpy as jnp
from jax import lax
from jax.experimental import pallas as pl
from jax.experimental.pallas import tpu as pltpu
from jax.sharding import PartitionSpec as P

HEADS = 16
HEAD_DIM = 64
PAGE = 8
LANES = 128
MESH = pl.DeviceIdType.MESH
BF16 = jnp.bfloat16
F32 = jnp.float32


def spans(col, qc, edge):
    low, high = col * qc, (col + 1) * qc
    cuts = [low] + ([edge] if low < edge < high else []) + [high]
    return list(zip(cuts[:-1], cuts[1:]))


def fused_kernel(dims, wq_ref, wo_ref, px_ref, tok_ref, dest_ref, seg_ref, gain_ref, bias_ref,
                 hid_ref, page_ref, gq_s, go_s, x_s, q_s, kv_s, attn_s, qm_s, km_s, out_s, in_s,
                 own_sem, w_recv, p_recv, oz_recv, o_recv, os_recv, w_z, w_x, w_y, w_xy, w_yx, w_s,
                 p_z, p_x, o_z, o_x, o_y, o_xy, o_s, t_send, t_recv):
    nz, nx, ny = dims
    n_row, n_col = nz * nx, ny * 2
    row, col = lax.axis_index("row"), lax.axis_index("col")
    z, x = row // nx, row % nx
    y, core = col // 2, col % 2
    rows, qc = wq_ref.shape
    oc = wo_ref.shape[1]
    prow = px_ref.shape[0]
    n_tok, width = tok_ref.shape
    n_pre = n_row * prow
    n_key = n_pre + n_tok
    slab = in_s.shape[1]
    cut = max(16, rows // 64 * 16)

    x_peers = [(x + d) % nx for d in range(1, nx)]
    y_peers = [(y + d) % ny for d in range(1, ny)]
    sibling = {"row": row, "col": y * 2 + 1 - core}
    up = {"row": jnp.minimum(z + 1, nz - 1) * nx + x, "col": col}
    down = {"row": jnp.maximum(z - 1, 0) * nx + x, "col": col}

    def to_x(d):
        return {"row": z * nx + x_peers[d], "col": col}

    def to_y(d):
        return {"row": row, "col": y_peers[d] * 2 + core}

    def remote(ref, send, recv, to):
        return pltpu.make_async_remote_copy(
            src_ref=ref, dst_ref=ref, send_sem=send, recv_sem=recv, device_id=to, device_id_type=MESH)

    def wblock(b, zb, a, part=None, side=None):
        c, r = b * 2 + (core if side is None else side), zb * nx + a
        first, count = {None: (0, rows), 0: (0, cut), 1: (cut, rows - cut)}[part]
        return gq_s.at[c, pl.ds(pl.multiple_of(r * rows + first, 16), count), :], w_recv.at[c, r]

    def w_copy(b, zb, a, send, to, part=None, side=None):
        ref, recv = wblock(b, zb, a, part, side)
        return remote(ref, send, recv, to)

    def wait_w(b, zb, a, side=None):
        w_copy(b, zb, a, w_s.at[0, 0], sibling, None, side).wait_recv()

    def x_send(zb, d):
        return w_copy(y, zb, x, w_x.at[d, zb], to_x(d))

    def y_send(zb, d):
        return w_copy(y, zb, x, w_y.at[d, zb], to_y(d))

    def xy_send(zb, i, d):
        return w_copy(y, zb, x_peers[i], w_xy.at[i, d, zb], to_y(d), 1)

    def yx_send(zb, j, d):
        return w_copy(y_peers[j], zb, x, w_yx.at[j, d, zb], to_x(d), 0)

    def s_send(b, zb, a):
        return w_copy(b, zb, a, w_s.at[b, zb * nx + a], sibling)

    def wz_send(zb, direction):
        return w_copy(y, zb, x, w_z.at[direction, zb], up if direction == 0 else down)

    def pblock(r):
        return x_s.at[pl.ds(pl.multiple_of(r * prow, prow), prow), :]

    def p_copy(r, send, to):
        return remote(pblock(r), send, p_recv.at[r], to)

    def wait_p(r):
        p_copy(r, w_s.at[0, 0], sibling).wait_recv()

    def pz_send(zb, direction):
        return p_copy(zb * nx + x, p_z.at[direction, zb], up if direction == 0 else down)

    def px_send(zb, d):
        return p_copy(zb * nx + x, p_x.at[d, zb], to_x(d))

    def oz_send(zb, direction):
        ref = go_s.at[col, zb, pl.ds(pl.multiple_of(x * rows, 16), rows), :]
        return remote(ref, o_z.at[direction, zb], oz_recv.at[zb], up if direction == 0 else down)

    def o_plane(b, a, side):
        return go_s.at[b * 2 + side, :, pl.ds(pl.multiple_of(a * rows, 16), rows), :]

    def o_copy(b, a, send, to):
        return remote(o_plane(b, a, core), send, o_recv.at[b, a], to)

    def ox_send(d):
        return o_copy(y, x, o_x.at[d], to_x(d))

    def oy_send(d):
        return o_copy(y, x, o_y.at[d], to_y(d))

    def oxy_send(i, d):
        return o_copy(y, x_peers[i], o_xy.at[i, d], to_y(d))

    def os_send(b, a):
        return remote(o_plane(b, a, core), o_s.at[b, a], os_recv.at[b, a], sibling)

    def wait_o(b, a):
        o_copy(b, a, o_s.at[0, 0], sibling).wait_recv()

    def wait_os(b, a):
        remote(o_plane(b, a, 1 - core), o_s.at[0, 0], os_recv.at[b, a], sibling).wait_recv()

    paired = nz & (nz - 1) == 0 and nx & (nx - 1) == 0
    offsets = [(dz, dx) for dx in range(nx) for dz in [0] + list(range(nz - 1, 0, -1))]

    def partner(k, sign):
        dz, dx = offsets[k]
        if paired:
            return (z ^ dz) * nx + (x ^ dx)
        return (z + sign * dz + nz) % nz * nx + (x + sign * dx + nx) % nx

    def t_copy(k):
        to = partner(k, 1)
        return pltpu.make_async_remote_copy(
            src_ref=out_s.at[to], dst_ref=in_s.at[k], send_sem=t_send.at[k],
            recv_sem=t_recv.at[k], device_id={"row": to, "col": col}, device_id_type=MESH)

    own = [
        pltpu.make_async_copy(wq_ref, wblock(y, z, x)[0], own_sem.at[0]),
        pltpu.make_async_copy(wo_ref, go_s.at[col, z, pl.ds(pl.multiple_of(x * rows, 16), rows), :],
                              own_sem.at[1]),
        pltpu.make_async_copy(px_ref, pblock(row), own_sem.at[2]),
    ]
    own_tok = pltpu.make_async_copy(tok_ref, x_s.at[pl.ds(n_pre, n_tok), :], own_sem.at[3])
    for copy in own:
        copy.start()
    own_tok.start()

    barrier = pltpu.get_barrier_semaphore()

    def greet(to):
        pl.semaphore_signal(barrier, inc=1, device_id=to, device_id_type=MESH)

    for d in range(1, n_row):
        greet({"row": (row + d) % n_row, "col": col})
    for d in range(ny - 1):
        greet(to_y(d))
    greet(sibling)
    pl.semaphore_wait(barrier, n_row + ny - 1)
    for copy in own:
        copy.wait()

    def at_distance(step, action):
        if step < 0 or step >= nz:
            return
        if step == 0:
            action(z, None)
            return

        @pl.when(z >= step)
        def _():
            action(z - step, 0)

        @pl.when(z + step < nz)
        def _():
            action(z + step, 1)

    def forward(send, zb, direction):
        if direction in (0, None):
            @pl.when(z < nz - 1)
            def _():
                send(zb, 0).start()
        if direction in (1, None):
            @pl.when(z > 0)
            def _():
                send(zb, 1).start()

    def from_z(zb, direction):
        if direction is not None:
            wait_w(y, zb, x)
        forward(wz_send, zb, direction)
        for d in range(nx - 1):
            x_send(zb, d).start()
        for d in range(ny - 1):
            y_send(zb, d).start()
        s_send(y, zb, x).start()

    def from_xy(zb, _):
        for i, a in enumerate(x_peers):
            wait_w(y, zb, a)
            for d in range(ny - 1):
                xy_send(zb, i, d).start()
            s_send(y, zb, a).start()
        for j, b in enumerate(y_peers):
            wait_w(b, zb, x)
            for d in range(nx - 1):
                yx_send(zb, j, d).start()
            s_send(b, zb, x).start()

    def from_diagonal(zb, _):
        for b in y_peers:
            for a in x_peers:
                wait_w(b, zb, a)
                s_send(b, zb, a).start()

    def prefix_from_z(zb, direction):
        if direction is not None:
            wait_p(zb * nx + x)
        forward(pz_send, zb, direction)
        for d in range(nx - 1):
            px_send(zb, d).start()

    def out_from_z(zb, direction):
        if direction is None:
            forward(oz_send, zb, direction)
            return

        @pl.when((z < nz - 1) if direction == 0 else (z > 0))
        def _():
            oz_send(zb, direction).wait_recv()
            oz_send(zb, direction).start()

    def out_rest(zb, direction):
        if direction is not None:
            @pl.when((z == nz - 1) if direction == 0 else (z == 0))
            def _():
                oz_send(zb, direction).wait_recv()

    at_distance(0, from_z)

    own_tok.wait()
    tokens = x_s.at[pl.ds(n_pre, n_tok), :]

    n_page = dest_ref.shape[1]
    most = slab // PAGE
    target = dest_ref[...].astype(F32)
    along = jnp.broadcast_to(target, (LANES, n_page)).T[:, :1]
    first_page = lax.broadcasted_iota(jnp.int32, (n_page, n_page), 0)
    second_page = lax.broadcasted_iota(jnp.int32, (n_page, n_page), 1)
    earlier = jnp.where((along == target) & (first_page < second_page), 1.0, 0.0)
    slot = target * most + jnp.sum(earlier, axis=0, keepdims=True)
    page_of = lax.broadcasted_iota(jnp.int32, (n_page, n_tok), 1) // PAGE
    member = jnp.where(page_of == lax.broadcasted_iota(jnp.int32, (n_page, n_tok), 0), 1.0, 0.0)
    slot_of = jnp.dot(jnp.broadcast_to(slot, (8, n_page)), member, precision=lax.Precision.HIGHEST,
                      preferred_element_type=F32)[:1]
    inside = lax.broadcasted_iota(jnp.int32, (1, n_tok), 1) % PAGE
    place = slot_of * PAGE + inside.astype(F32)

    def fill(i, _):
        first = i * slab
        want = lax.broadcasted_iota(jnp.int32, (slab, n_tok), 0) + first
        chosen = jnp.where(want.astype(F32) == place, 1.0, 0.0).astype(BF16)
        out_s[i] = jnp.dot(chosen, tokens[...], preferred_element_type=F32).astype(BF16)
        return 0

    lax.fori_loop(0, n_row, fill, 0)
    in_s[0] = out_s[row]

    for step in range(1, nz):
        at_distance(step, from_z)
        at_distance(step - 1, prefix_from_z)
        at_distance(step - 1, out_from_z)
    middle = (z == nz // 2) | (z == nz // 2 - 1)

    @pl.when(middle)
    def _():
        t_copy(1).start()

    at_distance(0, from_xy)
    at_distance(1, from_xy)
    at_distance(nz - 1, prefix_from_z)
    at_distance(nz - 1, out_from_z)
    for step in range(2, nz):
        at_distance(step, from_xy)
    @pl.when(jnp.logical_not(middle))
    def _():
        t_copy(1).start()

    for k in range(2, nz):
        t_copy(k).start()
    for step in range(1, nz):
        at_distance(step, out_rest)
    for d in range(nx - 1):
        ox_send(d).start()
    os_send(y, x).start()

    lane = lax.broadcasted_iota(jnp.int32, (n_tok, LANES), 1)
    low_half = lane < HEAD_DIM
    segment = jnp.broadcast_to(seg_ref[...].astype(F32), (LANES, n_tok)).T
    match = jnp.where(low_half, lane, lane - HEAD_DIM).astype(F32) == segment
    for half in range(2):
        part = low_half if half == 0 else jnp.logical_not(low_half)
        qm_s[half] = jnp.where(match, 0.0, jnp.where(part, -1e30, 0.0)).astype(BF16)
        km_s[half, n_pre:n_key, :] = jnp.where(match & part, 1.0, 0.0).astype(BF16)
        km_s[half, 0:n_pre, :] = jnp.zeros((n_pre, LANES), BF16)

    for zb in range(nz):
        for a in x_peers:
            wait_p(zb * nx + a)
    for zb in range(nz):
        for a in range(nx):
            wait_w(y, zb, a, 1 - core)

    low_of = []
    for c in range(n_col):
        low_of.append(spans(c, qc, width))

    def project(c):
        for low, high in low_of[c]:
            w = gq_s[c, :, low - c * qc:high - c * qc]
            if high <= width:
                q_s[:, low:high] = (jnp.dot(tokens[...], w, preferred_element_type=F32)
                                    * HEAD_DIM ** (-0.5)).astype(BF16)
            else:
                kv_s[:, low - width:high - width] = jnp.dot(
                    x_s[...], w, preferred_element_type=F32).astype(BF16)

    def project_side(b):
        for side in range(2):
            project(b * 2 + side)

    for b in range(ny):
        @pl.when(y == b)
        def _():
            project_side(b)

    for k in range(nz, n_row):
        t_copy(k).start()
    for step in range(nz):
        at_distance(step, from_diagonal)
    for b in y_peers:
        for zb in range(nz):
            for a in range(nx):
                wait_w(b, zb, a, 1 - core)
    for d in range(ny - 1):
        oy_send(d).start()

    for b in range(ny):
        @pl.when(y != b)
        def _():
            project_side(b)

    lane_row = lax.broadcasted_iota(jnp.int32, (1, LANES), 1)
    keep = [jnp.where(lane_row < HEAD_DIM, 1.0, 0.0).astype(BF16),
            jnp.where(lane_row < HEAD_DIM, 0.0, 1.0).astype(BF16)]
    tile = min(256, n_tok)

    def pair(j, _):
        @pl.when(j == 1)
        def _():
            for i, a in enumerate(x_peers):
                wait_o(y, a)
                for d in range(ny - 1):
                    oxy_send(i, d).start()
                os_send(y, a).start()

        @pl.when(j == 3)
        def _():
            for b in y_peers:
                wait_o(b, x)
                os_send(b, x).start()

        @pl.when(j == 5)
        def _():
            for b in y_peers:
                for a in x_peers:
                    wait_o(b, a)
                    os_send(b, a).start()

        cols = pl.ds(pl.multiple_of(j * LANES, LANES), LANES)
        vcols = pl.ds(pl.multiple_of(width + j * LANES, LANES), LANES)
        keys = kv_s[:, cols]
        values = kv_s[:, vcols]
        k_aug = [keys * keep[h] + km_s[1 - h] for h in range(2)]
        v_aug = [values * keep[h] + keep[1 - h] for h in range(2)]
        chains = [(t, h) for t in range(n_tok // tile) for h in range(2)]
        scores, outs = {}, {}

        def score(t, h):
            span = slice(t * tile, (t + 1) * tile)
            q_aug = q_s[span, cols] * keep[h] + qm_s[1 - h, span, :]
            scores[t, h] = lax.dot_general(q_aug, k_aug[h], (((1,), (1,)), ((), ())),
                                           preferred_element_type=F32)

        def weigh(t, h):
            s = scores[t, h]
            m = jnp.max(s, axis=-1, keepdims=True)
            outs[t, h] = jnp.dot(jnp.exp(s - m).astype(BF16), v_aug[h], preferred_element_type=F32)

        score(*chains[0])
        for i, chain in enumerate(chains):
            if i + 1 < len(chains):
                score(*chains[i + 1])
            weigh(*chain)
        first = lax.broadcasted_iota(jnp.int32, (tile, LANES), 1) < HEAD_DIM
        for t in range(n_tok // tile):
            num = jnp.where(first, outs[t, 0], outs[t, 1])
            total = pltpu.roll(jnp.where(first, outs[t, 1], outs[t, 0]), HEAD_DIM, 1)
            attn_s[t * tile:(t + 1) * tile, cols] = (num / total).astype(BF16)
        return 0

    lax.fori_loop(0, width // LANES, pair, 0)

    for b in range(ny):
        for a in range(nx):
            wait_os(b, a)
    for t in range(n_tok // tile):
        span = slice(t * tile, (t + 1) * tile)
        a = attn_s[span, :]
        mixed = tokens[span, :].astype(F32) + jnp.concatenate(
            [jnp.dot(a, go_s[c].reshape(n_row * rows, oc), preferred_element_type=F32)
             for c in range(n_col)], axis=1)
        center = jnp.mean(mixed, axis=-1, keepdims=True)
        off = mixed - center
        spread_of = jnp.mean(off * off, axis=-1, keepdims=True)
        hid_ref[span, :] = (off * lax.rsqrt(spread_of + 1e-05) * gain_ref[...] + bias_ref[...]).astype(BF16)

    group = max(1, min(n_row, 256 // slab))

    for i in range(n_row // group):
        members = range(i * group, (i + 1) * group)
        for k in members:
            if k:
                t_copy(k).wait_recv()
        some = in_s[i * group:(i + 1) * group].reshape(group * slab, width)
        for c in range(n_col):
            for low, high in low_of[c]:
                if low >= width:
                    made = jnp.dot(some, gq_s[c, :, low - c * qc:high - c * qc],
                                   preferred_element_type=F32).astype(BF16)
                    for j, k in enumerate(members):
                        page_ref[partner(k, -1), :, low - width:high - width] = made[j * slab:(j + 1) * slab]

    for zb in range(nz):
        @pl.when((z < nz - 1) & (zb <= z))
        def _():
            for send in (wz_send, pz_send, oz_send):
                send(zb, 0).wait_send()

        @pl.when((z > 0) & (zb >= z))
        def _():
            for send in (wz_send, pz_send, oz_send):
                send(zb, 1).wait_send()

        for d in range(nx - 1):
            x_send(zb, d).wait_send()
            px_send(zb, d).wait_send()
            for j in range(ny - 1):
                yx_send(zb, j, d).wait_send()
        for d in range(ny - 1):
            y_send(zb, d).wait_send()
            for i in range(nx - 1):
                xy_send(zb, i, d).wait_send()
        for b in range(ny):
            for a in range(nx):
                s_send(b, zb, a).wait_send()
    for d in range(nx - 1):
        ox_send(d).wait_send()
    for d in range(ny - 1):
        oy_send(d).wait_send()
        for i in range(nx - 1):
            oxy_send(i, d).wait_send()
    for b in range(ny):
        for a in range(nx):
            os_send(b, a).wait_send()
    for k in range(1, n_row):
        t_copy(k).wait_send()


def fused(dims, w_qkv, w_out, prefix, tokens, dest, segment, gain, bias, slab):
    nz, nx, ny = dims
    n_row, n_col = nz * nx, ny * 2
    rows, qc = w_qkv.shape
    oc = w_out.shape[1]
    prow, width = prefix.shape
    n_tok = tokens.shape[0]
    n_pre = n_row * prow
    n_key = n_pre + n_tok
    dma = pltpu.SemaphoreType.DMA
    anywhere = pl.BlockSpec(memory_space=pl.ANY)
    vmem = pl.BlockSpec(memory_space=pltpu.VMEM)
    xs, ys = max(1, nx - 1), max(1, ny - 1)
    return pl.pallas_call(
        functools.partial(fused_kernel, dims),
        out_shape=(pltpu.VMEM((n_tok, width), BF16),
                   pltpu.VMEM((n_row, slab, 2 * width), BF16)),
        in_specs=[anywhere] * 4 + [vmem] * 4,
        out_specs=(vmem, vmem),
        scratch_shapes=[
            pltpu.VMEM((n_col, n_row * rows, qc), BF16),
            pltpu.VMEM((n_col, nz, nx * rows, oc), BF16),
            pltpu.VMEM((n_key, width), BF16),
            pltpu.VMEM((n_tok, width), BF16),
            pltpu.VMEM((n_key, 2 * width), BF16),
            pltpu.VMEM((n_tok, width), BF16),
            pltpu.VMEM((2, n_tok, LANES), BF16),
            pltpu.VMEM((2, n_key, LANES), BF16),
            pltpu.VMEM((n_row, slab, width), BF16),
            pltpu.VMEM((n_row, slab, width), BF16),
            dma((4,)), dma((n_col, n_row)), dma((n_row,)), dma((nz,)), dma((ny, nx)), dma((ny, nx)),
            dma((2, nz)), dma((xs, nz)), dma((ys, nz)), dma((xs, ys, nz)), dma((ys, xs, nz)), dma((ny, n_row)),
            dma((2, nz)), dma((xs, nz)), dma((2, nz)), dma((xs,)), dma((ys,)), dma((xs, ys)), dma((ny, nx)),
            dma((n_row,)), dma((n_row,))],
        compiler_params=pltpu.CompilerParams(
            collective_id=0, has_side_effects=True, vmem_limit_bytes=54 * 1024 * 1024),
        name="fused",
    )(w_qkv, w_out, prefix, tokens, dest, segment, gain, bias)


def settle_kernel(parts, hid_ref, page_ref, hid_out, page_out, sem):
    n = page_ref.shape[0]
    step = n // parts
    copies = [pltpu.make_async_copy(page_ref.at[pl.ds(i * step, step)], page_out.at[pl.ds(i * step, step)], sem.at[i])
              for i in range(parts)]
    copies.append(pltpu.make_async_copy(hid_ref, hid_out, sem.at[parts]))
    for copy in copies:
        copy.start()
    for copy in copies:
        copy.wait()


def settle(hidden, pages):
    anywhere = pl.BlockSpec(memory_space=pl.ANY)
    parts = min(8, pages.shape[0])
    return pl.pallas_call(
        functools.partial(settle_kernel, parts),
        out_shape=(jax.ShapeDtypeStruct(hidden.shape, BF16), jax.ShapeDtypeStruct(pages.shape, BF16)),
        in_specs=[anywhere] * 2,
        out_specs=(pl.BlockSpec(memory_space=pltpu.HBM),) * 2,
        scratch_shapes=[pltpu.SemaphoreType.DMA((parts + 1,))],
        compiler_params=pltpu.CompilerParams(vmem_limit_bytes=1024 * 1024),
        name="settle",
    )(hidden, pages)


def local(dims, suffix_x, segment_ids, prefix_x, w_qkv, w_out, norm_gain, norm_bias, page_dest):
    width = suffix_x.shape[-1]
    tokens = suffix_x[0, 0]
    n_tok = tokens.shape[0]
    ranks = lax.axis_size("row")
    pages_dev = n_tok // PAGE
    most = max(2, 2 * pages_dev // ranks)
    hidden, pages = fused(dims, w_qkv, w_out, prefix_x[0], tokens, page_dest[0, 0].reshape(1, pages_dev),
                          segment_ids[0], norm_gain[None], norm_bias[None], most * PAGE)
    hidden, pages = settle(hidden, pages)
    pages = pages.reshape(ranks, most, PAGE, 2 * width)
    return (hidden[None, None], pages[None, None])


def solution(mesh):
    n_row, n_col = mesh.shape["row"], mesh.shape["col"]
    ny = n_col // 2
    nx = ny if n_row % ny == 0 else 1
    dims = (n_row // nx, nx, ny)
    in_specs = (
        P("col", "row", None, None),
        P("col", "row", None),
        P("col", "row", None),
        P("row", "col"),
        P("row", "col"),
        P(),
        P(),
        P("col", "row", None, None),
    )
    out_specs = (P("col", "row", None, None), P("col", "row", None, None, None, None))
    return jax.shard_map(functools.partial(local, dims), mesh=mesh, in_specs=in_specs,
                         out_specs=out_specs, check_vma=False)
```

```python
import functools

import jax
import jax.numpy as jnp
from jax import lax
from jax.experimental import pallas as pl
from jax.experimental.pallas import tpu as pltpu
from jax.sharding import PartitionSpec as P

HEADS = 16
HEAD_DIM = 64
PAGE = 8
LANES = 128
MESH = pl.DeviceIdType.MESH
BF16 = jnp.bfloat16
F32 = jnp.float32


def spans(col, qc, edge):
    low, high = col * qc, (col + 1) * qc
    cuts = [low] + ([edge] if low < edge < high else []) + [high]
    return list(zip(cuts[:-1], cuts[1:]))


def fused_kernel(dims, wq_ref, wo_ref, px_ref, tok_ref, dest_ref, seg_ref, gain_ref, bias_ref,
                 hid_ref, page_ref, gq_s, go_s, x_s, q_s, kv_s, attn_s, qm_s, km_s, out_s, in_s,
                 own_sem, w_recv, p_recv, oz_recv, o_recv, os_recv, w_z, w_x, w_y, w_xy, w_yx, w_s,
                 p_z, p_x, o_z, o_x, o_y, o_xy, o_s, t_send, t_recv):
    nz, nx, ny = dims
    n_row, n_col = nz * nx, ny * 2
    row, col = lax.axis_index("row"), lax.axis_index("col")
    z, x = row // nx, row % nx
    y, core = col // 2, col % 2
    rows, qc = wq_ref.shape
    oc = wo_ref.shape[1]
    prow = px_ref.shape[0]
    n_tok, width = tok_ref.shape
    n_pre = n_row * prow
    n_key = n_pre + n_tok
    slab = in_s.shape[1]
    cut = max(16, rows // 64 * 16)

    x_peers = [(x + d) % nx for d in range(1, nx)]
    y_peers = [(y + d) % ny for d in range(1, ny)]
    sibling = {"row": row, "col": y * 2 + 1 - core}
    up = {"row": jnp.minimum(z + 1, nz - 1) * nx + x, "col": col}
    down = {"row": jnp.maximum(z - 1, 0) * nx + x, "col": col}

    def to_x(d):
        return {"row": z * nx + x_peers[d], "col": col}

    def to_y(d):
        return {"row": row, "col": y_peers[d] * 2 + core}

    def remote(ref, send, recv, to):
        return pltpu.make_async_remote_copy(
            src_ref=ref, dst_ref=ref, send_sem=send, recv_sem=recv, device_id=to, device_id_type=MESH)

    def wblock(b, zb, a, part=None, side=None):
        c, r = b * 2 + (core if side is None else side), zb * nx + a
        first, count = {None: (0, rows), 0: (0, cut), 1: (cut, rows - cut)}[part]
        return gq_s.at[c, pl.ds(pl.multiple_of(r * rows + first, 16), count), :], w_recv.at[c, r]

    def w_copy(b, zb, a, send, to, part=None, side=None):
        ref, recv = wblock(b, zb, a, part, side)
        return remote(ref, send, recv, to)

    def wait_w(b, zb, a, side=None):
        w_copy(b, zb, a, w_s.at[0, 0], sibling, None, side).wait_recv()

    def x_send(zb, d):
        return w_copy(y, zb, x, w_x.at[d, zb], to_x(d))

    def y_send(zb, d):
        return w_copy(y, zb, x, w_y.at[d, zb], to_y(d))

    def xy_send(zb, i, d):
        return w_copy(y, zb, x_peers[i], w_xy.at[i, d, zb], to_y(d), 1)

    def yx_send(zb, j, d):
        return w_copy(y_peers[j], zb, x, w_yx.at[j, d, zb], to_x(d), 0)

    def s_send(b, zb, a):
        return w_copy(b, zb, a, w_s.at[b, zb * nx + a], sibling)

    def wz_send(zb, direction):
        return w_copy(y, zb, x, w_z.at[direction, zb], up if direction == 0 else down)

    def pblock(r):
        return x_s.at[pl.ds(pl.multiple_of(r * prow, prow), prow), :]

    def p_copy(r, send, to):
        return remote(pblock(r), send, p_recv.at[r], to)

    def wait_p(r):
        p_copy(r, w_s.at[0, 0], sibling).wait_recv()

    def pz_send(zb, direction):
        return p_copy(zb * nx + x, p_z.at[direction, zb], up if direction == 0 else down)

    def px_send(zb, d):
        return p_copy(zb * nx + x, p_x.at[d, zb], to_x(d))

    def oz_send(zb, direction):
        ref = go_s.at[col, zb, pl.ds(pl.multiple_of(x * rows, 16), rows), :]
        return remote(ref, o_z.at[direction, zb], oz_recv.at[zb], up if direction == 0 else down)

    def o_plane(b, a, side):
        return go_s.at[b * 2 + side, :, pl.ds(pl.multiple_of(a * rows, 16), rows), :]

    def o_copy(b, a, send, to):
        return remote(o_plane(b, a, core), send, o_recv.at[b, a], to)

    def ox_send(d):
        return o_copy(y, x, o_x.at[d], to_x(d))

    def oy_send(d):
        return o_copy(y, x, o_y.at[d], to_y(d))

    def oxy_send(i, d):
        return o_copy(y, x_peers[i], o_xy.at[i, d], to_y(d))

    def os_send(b, a):
        return remote(o_plane(b, a, core), o_s.at[b, a], os_recv.at[b, a], sibling)

    def wait_o(b, a):
        o_copy(b, a, o_s.at[0, 0], sibling).wait_recv()

    def wait_os(b, a):
        remote(o_plane(b, a, 1 - core), o_s.at[0, 0], os_recv.at[b, a], sibling).wait_recv()

    paired = nz & (nz - 1) == 0 and nx & (nx - 1) == 0
    offsets = [(dz, dx) for dx in range(nx) for dz in [0] + list(range(nz - 1, 0, -1))]

    def partner(k, sign):
        dz, dx = offsets[k]
        if paired:
            return (z ^ dz) * nx + (x ^ dx)
        return (z + sign * dz + nz) % nz * nx + (x + sign * dx + nx) % nx

    def t_copy(k):
        to = partner(k, 1)
        return pltpu.make_async_remote_copy(
            src_ref=out_s.at[to], dst_ref=in_s.at[k], send_sem=t_send.at[k],
            recv_sem=t_recv.at[k], device_id={"row": to, "col": col}, device_id_type=MESH)

    own = [
        pltpu.make_async_copy(wq_ref, wblock(y, z, x)[0], own_sem.at[0]),
        pltpu.make_async_copy(wo_ref, go_s.at[col, z, pl.ds(pl.multiple_of(x * rows, 16), rows), :],
                              own_sem.at[1]),
        pltpu.make_async_copy(px_ref, pblock(row), own_sem.at[2]),
    ]
    own_tok = pltpu.make_async_copy(tok_ref, x_s.at[pl.ds(n_pre, n_tok), :], own_sem.at[3])
    for copy in own:
        copy.start()
    own_tok.start()

    barrier = pltpu.get_barrier_semaphore()

    def greet(to):
        pl.semaphore_signal(barrier, inc=1, device_id=to, device_id_type=MESH)

    for d in range(1, n_row):
        greet({"row": (row + d) % n_row, "col": col})
    for d in range(ny - 1):
        greet(to_y(d))
    greet(sibling)
    pl.semaphore_wait(barrier, n_row + ny - 1)
    for copy in own:
        copy.wait()

    def at_distance(step, action):
        if step < 0 or step >= nz:
            return
        if step == 0:
            action(z, None)
            return

        @pl.when(z >= step)
        def _():
            action(z - step, 0)

        @pl.when(z + step < nz)
        def _():
            action(z + step, 1)

    def forward(send, zb, direction):
        if direction in (0, None):
            @pl.when(z < nz - 1)
            def _():
                send(zb, 0).start()
        if direction in (1, None):
            @pl.when(z > 0)
            def _():
                send(zb, 1).start()

    def from_z(zb, direction):
        if direction is not None:
            wait_w(y, zb, x)
        forward(wz_send, zb, direction)
        for d in range(nx - 1):
            x_send(zb, d).start()
        for d in range(ny - 1):
            y_send(zb, d).start()
        s_send(y, zb, x).start()

    def from_xy(zb, _):
        for i, a in enumerate(x_peers):
            wait_w(y, zb, a)
            for d in range(ny - 1):
                xy_send(zb, i, d).start()
            s_send(y, zb, a).start()
        for j, b in enumerate(y_peers):
            wait_w(b, zb, x)
            for d in range(nx - 1):
                yx_send(zb, j, d).start()
            s_send(b, zb, x).start()

    def from_diagonal(zb, _):
        for b in y_peers:
            for a in x_peers:
                wait_w(b, zb, a)
                s_send(b, zb, a).start()

    def prefix_from_z(zb, direction):
        if direction is not None:
            wait_p(zb * nx + x)
        forward(pz_send, zb, direction)
        for d in range(nx - 1):
            px_send(zb, d).start()

    def out_from_z(zb, direction):
        if direction is None:
            forward(oz_send, zb, direction)
            return

        @pl.when((z < nz - 1) if direction == 0 else (z > 0))
        def _():
            oz_send(zb, direction).wait_recv()
            oz_send(zb, direction).start()

    def out_rest(zb, direction):
        if direction is not None:
            @pl.when((z == nz - 1) if direction == 0 else (z == 0))
            def _():
                oz_send(zb, direction).wait_recv()

    at_distance(0, from_z)

    own_tok.wait()
    tokens = x_s.at[pl.ds(n_pre, n_tok), :]

    n_page = dest_ref.shape[1]
    most = slab // PAGE
    target = dest_ref[...].astype(F32)
    along = jnp.broadcast_to(target, (LANES, n_page)).T[:, :1]
    first_page = lax.broadcasted_iota(jnp.int32, (n_page, n_page), 0)
    second_page = lax.broadcasted_iota(jnp.int32, (n_page, n_page), 1)
    earlier = jnp.where((along == target) & (first_page < second_page), 1.0, 0.0)
    slot = target * most + jnp.sum(earlier, axis=0, keepdims=True)
    page_of = lax.broadcasted_iota(jnp.int32, (n_page, n_tok), 1) // PAGE
    member = jnp.where(page_of == lax.broadcasted_iota(jnp.int32, (n_page, n_tok), 0), 1.0, 0.0)
    slot_of = jnp.dot(jnp.broadcast_to(slot, (8, n_page)), member, precision=lax.Precision.HIGHEST,
                      preferred_element_type=F32)[:1]
    inside = lax.broadcasted_iota(jnp.int32, (1, n_tok), 1) % PAGE
    place = slot_of * PAGE + inside.astype(F32)

    def fill(i, _):
        first = i * slab
        want = lax.broadcasted_iota(jnp.int32, (slab, n_tok), 0) + first
        chosen = jnp.where(want.astype(F32) == place, 1.0, 0.0).astype(BF16)
        out_s[i] = jnp.dot(chosen, tokens[...], preferred_element_type=F32).astype(BF16)
        return 0

    lax.fori_loop(0, n_row, fill, 0)
    in_s[0] = out_s[row]

    for step in range(1, nz):
        at_distance(step, from_z)
        at_distance(step - 1, prefix_from_z)
        at_distance(step - 1, out_from_z)
    middle = (z == nz // 2) | (z == nz // 2 - 1)

    @pl.when(middle)
    def _():
        t_copy(1).start()

    at_distance(0, from_xy)
    at_distance(1, from_xy)
    at_distance(nz - 1, prefix_from_z)
    at_distance(nz - 1, out_from_z)
    for step in range(2, nz):
        at_distance(step, from_xy)
    @pl.when(jnp.logical_not(middle))
    def _():
        t_copy(1).start()

    for k in range(2, nz):
        t_copy(k).start()
    for step in range(1, nz):
        at_distance(step, out_rest)
    for d in range(nx - 1):
        ox_send(d).start()
    os_send(y, x).start()

    lane = lax.broadcasted_iota(jnp.int32, (n_tok, LANES), 1)
    low_half = lane < HEAD_DIM
    segment = jnp.broadcast_to(seg_ref[...].astype(F32), (LANES, n_tok)).T
    match = jnp.where(low_half, lane, lane - HEAD_DIM).astype(F32) == segment
    for half in range(2):
        part = low_half if half == 0 else jnp.logical_not(low_half)
        qm_s[half] = jnp.where(match, 0.0, jnp.where(part, -1e30, 0.0)).astype(BF16)
        km_s[half, n_pre:n_key, :] = jnp.where(match & part, 1.0, 0.0).astype(BF16)
        km_s[half, 0:n_pre, :] = jnp.zeros((n_pre, LANES), BF16)

    for zb in range(nz):
        for a in x_peers:
            wait_p(zb * nx + a)
    for zb in range(nz):
        for a in range(nx):
            wait_w(y, zb, a, 1 - core)

    low_of = []
    for c in range(n_col):
        low_of.append(spans(c, qc, width))

    def project(c):
        for low, high in low_of[c]:
            w = gq_s[c, :, low - c * qc:high - c * qc]
            if high <= width:
                q_s[:, low:high] = (jnp.dot(tokens[...], w, preferred_element_type=F32)
                                    * HEAD_DIM ** (-0.5)).astype(BF16)
            else:
                kv_s[:, low - width:high - width] = jnp.dot(
                    x_s[...], w, preferred_element_type=F32).astype(BF16)

    def project_side(b):
        for side in range(2):
            project(b * 2 + side)

    for b in range(ny):
        @pl.when(y == b)
        def _():
            project_side(b)

    for k in range(nz, n_row):
        t_copy(k).start()
    for step in range(nz):
        at_distance(step, from_diagonal)
    for b in y_peers:
        for zb in range(nz):
            for a in range(nx):
                wait_w(b, zb, a, 1 - core)
    for d in range(ny - 1):
        oy_send(d).start()

    for b in range(ny):
        @pl.when(y != b)
        def _():
            project_side(b)

    lane_row = lax.broadcasted_iota(jnp.int32, (1, LANES), 1)
    keep = [jnp.where(lane_row < HEAD_DIM, 1.0, 0.0).astype(BF16),
            jnp.where(lane_row < HEAD_DIM, 0.0, 1.0).astype(BF16)]
    tile = min(256, n_tok)

    def pair(j, _):
        @pl.when(j == 1)
        def _():
            for i, a in enumerate(x_peers):
                wait_o(y, a)
                for d in range(ny - 1):
                    oxy_send(i, d).start()
                os_send(y, a).start()

        @pl.when(j == 3)
        def _():
            for b in y_peers:
                wait_o(b, x)
                os_send(b, x).start()

        @pl.when(j == 5)
        def _():
            for b in y_peers:
                for a in x_peers:
                    wait_o(b, a)
                    os_send(b, a).start()

        cols = pl.ds(pl.multiple_of(j * LANES, LANES), LANES)
        vcols = pl.ds(pl.multiple_of(width + j * LANES, LANES), LANES)
        keys = kv_s[:, cols]
        values = kv_s[:, vcols]
        k_aug = [keys * keep[h] + km_s[1 - h] for h in range(2)]
        v_aug = [values * keep[h] + keep[1 - h] for h in range(2)]
        chains = [(t, h) for t in range(n_tok // tile) for h in range(2)]
        scores, outs = {}, {}

        def score(t, h):
            span = slice(t * tile, (t + 1) * tile)
            q_aug = q_s[span, cols] * keep[h] + qm_s[1 - h, span, :]
            scores[t, h] = lax.dot_general(q_aug, k_aug[h], (((1,), (1,)), ((), ())),
                                           preferred_element_type=F32)

        def weigh(t, h):
            s = scores[t, h]
            m = jnp.max(s, axis=-1, keepdims=True)
            outs[t, h] = jnp.dot(jnp.exp(s - m).astype(BF16), v_aug[h], preferred_element_type=F32)

        score(*chains[0])
        for i, chain in enumerate(chains):
            if i + 1 < len(chains):
                score(*chains[i + 1])
            weigh(*chain)
        first = lax.broadcasted_iota(jnp.int32, (tile, LANES), 1) < HEAD_DIM
        for t in range(n_tok // tile):
            num = jnp.where(first, outs[t, 0], outs[t, 1])
            total = pltpu.roll(jnp.where(first, outs[t, 1], outs[t, 0]), HEAD_DIM, 1)
            attn_s[t * tile:(t + 1) * tile, cols] = (num / total).astype(BF16)
        return 0

    lax.fori_loop(0, width // LANES, pair, 0, unroll=2)

    for b in range(ny):
        for a in range(nx):
            wait_os(b, a)
    for t in range(n_tok // tile):
        span = slice(t * tile, (t + 1) * tile)
        a = attn_s[span, :]
        mixed = tokens[span, :].astype(F32) + jnp.concatenate(
            [jnp.dot(a, go_s[c].reshape(n_row * rows, oc), preferred_element_type=F32)
             for c in range(n_col)], axis=1)
        center = jnp.mean(mixed, axis=-1, keepdims=True)
        off = mixed - center
        spread_of = jnp.mean(off * off, axis=-1, keepdims=True)
        hid_ref[span, :] = (off * lax.rsqrt(spread_of + 1e-05) * gain_ref[...] + bias_ref[...]).astype(BF16)

    group = max(1, min(n_row, 256 // slab))

    for i in range(n_row // group):
        members = range(i * group, (i + 1) * group)
        for k in members:
            if k:
                t_copy(k).wait_recv()
        some = in_s[i * group:(i + 1) * group].reshape(group * slab, width)
        for c in range(n_col):
            for low, high in low_of[c]:
                if low >= width:
                    made = jnp.dot(some, gq_s[c, :, low - c * qc:high - c * qc],
                                   preferred_element_type=F32).astype(BF16)
                    for j, k in enumerate(members):
                        page_ref[partner(k, -1), :, low - width:high - width] = made[j * slab:(j + 1) * slab]

    for zb in range(nz):
        @pl.when((z < nz - 1) & (zb <= z))
        def _():
            for send in (wz_send, pz_send, oz_send):
                send(zb, 0).wait_send()

        @pl.when((z > 0) & (zb >= z))
        def _():
            for send in (wz_send, pz_send, oz_send):
                send(zb, 1).wait_send()

        for d in range(nx - 1):
            x_send(zb, d).wait_send()
            px_send(zb, d).wait_send()
            for j in range(ny - 1):
                yx_send(zb, j, d).wait_send()
        for d in range(ny - 1):
            y_send(zb, d).wait_send()
            for i in range(nx - 1):
                xy_send(zb, i, d).wait_send()
        for b in range(ny):
            for a in range(nx):
                s_send(b, zb, a).wait_send()
    for d in range(nx - 1):
        ox_send(d).wait_send()
    for d in range(ny - 1):
        oy_send(d).wait_send()
        for i in range(nx - 1):
            oxy_send(i, d).wait_send()
    for b in range(ny):
        for a in range(nx):
            os_send(b, a).wait_send()
    for k in range(1, n_row):
        t_copy(k).wait_send()


def fused(dims, w_qkv, w_out, prefix, tokens, dest, segment, gain, bias, slab):
    nz, nx, ny = dims
    n_row, n_col = nz * nx, ny * 2
    rows, qc = w_qkv.shape
    oc = w_out.shape[1]
    prow, width = prefix.shape
    n_tok = tokens.shape[0]
    n_pre = n_row * prow
    n_key = n_pre + n_tok
    dma = pltpu.SemaphoreType.DMA
    anywhere = pl.BlockSpec(memory_space=pl.ANY)
    vmem = pl.BlockSpec(memory_space=pltpu.VMEM)
    xs, ys = max(1, nx - 1), max(1, ny - 1)
    return pl.pallas_call(
        functools.partial(fused_kernel, dims),
        out_shape=(pltpu.VMEM((n_tok, width), BF16),
                   pltpu.VMEM((n_row, slab, 2 * width), BF16)),
        in_specs=[anywhere] * 4 + [vmem] * 4,
        out_specs=(vmem, vmem),
        scratch_shapes=[
            pltpu.VMEM((n_col, n_row * rows, qc), BF16),
            pltpu.VMEM((n_col, nz, nx * rows, oc), BF16),
            pltpu.VMEM((n_key, width), BF16),
            pltpu.VMEM((n_tok, width), BF16),
            pltpu.VMEM((n_key, 2 * width), BF16),
            pltpu.VMEM((n_tok, width), BF16),
            pltpu.VMEM((2, n_tok, LANES), BF16),
            pltpu.VMEM((2, n_key, LANES), BF16),
            pltpu.VMEM((n_row, slab, width), BF16),
            pltpu.VMEM((n_row, slab, width), BF16),
            dma((4,)), dma((n_col, n_row)), dma((n_row,)), dma((nz,)), dma((ny, nx)), dma((ny, nx)),
            dma((2, nz)), dma((xs, nz)), dma((ys, nz)), dma((xs, ys, nz)), dma((ys, xs, nz)), dma((ny, n_row)),
            dma((2, nz)), dma((xs, nz)), dma((2, nz)), dma((xs,)), dma((ys,)), dma((xs, ys)), dma((ny, nx)),
            dma((n_row,)), dma((n_row,))],
        compiler_params=pltpu.CompilerParams(
            collective_id=0, has_side_effects=True, vmem_limit_bytes=54 * 1024 * 1024),
        name="fused",
    )(w_qkv, w_out, prefix, tokens, dest, segment, gain, bias)


def settle_kernel(parts, hid_ref, page_ref, hid_out, page_out, sem):
    n = page_ref.shape[0]
    step = n // parts
    copies = [pltpu.make_async_copy(page_ref.at[pl.ds(i * step, step)], page_out.at[pl.ds(i * step, step)], sem.at[i])
              for i in range(parts)]
    copies.append(pltpu.make_async_copy(hid_ref, hid_out, sem.at[parts]))
    for copy in copies:
        copy.start()
    for copy in copies:
        copy.wait()


def settle(hidden, pages):
    anywhere = pl.BlockSpec(memory_space=pl.ANY)
    parts = min(8, pages.shape[0])
    return pl.pallas_call(
        functools.partial(settle_kernel, parts),
        out_shape=(jax.ShapeDtypeStruct(hidden.shape, BF16), jax.ShapeDtypeStruct(pages.shape, BF16)),
        in_specs=[anywhere] * 2,
        out_specs=(pl.BlockSpec(memory_space=pltpu.HBM),) * 2,
        scratch_shapes=[pltpu.SemaphoreType.DMA((parts + 1,))],
        compiler_params=pltpu.CompilerParams(vmem_limit_bytes=1024 * 1024),
        name="settle",
    )(hidden, pages)


def local(dims, suffix_x, segment_ids, prefix_x, w_qkv, w_out, norm_gain, norm_bias, page_dest):
    width = suffix_x.shape[-1]
    tokens = suffix_x[0, 0]
    n_tok = tokens.shape[0]
    ranks = lax.axis_size("row")
    pages_dev = n_tok // PAGE
    most = max(2, 2 * pages_dev // ranks)
    hidden, pages = fused(dims, w_qkv, w_out, prefix_x[0], tokens, page_dest[0, 0].reshape(1, pages_dev),
                          segment_ids[0], norm_gain[None], norm_bias[None], most * PAGE)
    hidden, pages = settle(hidden, pages)
    pages = pages.reshape(ranks, most, PAGE, 2 * width)
    return (hidden[None, None], pages[None, None])


def solution(mesh):
    n_row, n_col = mesh.shape["row"], mesh.shape["col"]
    ny = n_col // 2
    nx = ny if n_row % ny == 0 else 1
    dims = (n_row // nx, nx, ny)
    in_specs = (
        P("col", "row", None, None),
        P("col", "row", None),
        P("col", "row", None),
        P("row", "col"),
        P("row", "col"),
        P(),
        P(),
        P("col", "row", None, None),
    )
    out_specs = (P("col", "row", None, None), P("col", "row", None, None, None, None))
    return jax.shard_map(functools.partial(local, dims), mesh=mesh, in_specs=in_specs,
                         out_specs=out_specs, check_vma=False)
```
